256 devices in a mesh: obj: 32 (over x, z_hi, core), ep: 8 (over z_lo, y).
Axes of the slice: x: 4, y: 4, z: 8 (z_hi: 4, z_lo: 2; z = z_hi * 2 + z_lo), core: 2. Of those that a mesh axis runs over, the one named last changes fastest.
Arguments:
- light_curves: float32 [4096, 1024], P('obj', 'ep'), may hold values from -40 to 40
- valid: int32 [4096, 1024], P('obj', 'ep'), may hold values 0 or 1
- pixel: int32 [4096], P('obj'), may hold values from 0 to 127, never falling along the last dimension, each value on 1 to 64 neighbouring positions
- inv_sigma: float32 [4096], P('obj'), may hold values from 0.5 to 4
- modes_init: float32 [1024, 16], P('ep'), may hold values from -6 to 6
- epoch_jitter: float32 [1024], replicated, may hold values from 0 to 0.9
- freq_index: int32 [2048], replicated, may hold values from 4 to 2047
Outputs:
- residual: float32 [4096, 1024], P('obj', 'ep')
- power: float32 [4096, 2048], P(('obj', 'ep'))
The draws below stay inside these ranges and needn't reach their ends.
Inputs may be any that keep to these rules, and one draw needn't show every extreme that they name: Pixels never decrease along the objects; each pixel holds 1 to 64 objects, and some pixel exactly 64.
All inputs are finite; a program needn't handle non-finite values. No bound on the sum of `valid` on one device may be relied on, other than what follows from the above.
Results may differ from the reference program's by a relative error of at most 0.0052.
Values may be sent and summed in bfloat16 or wider, within the bound.
No kernel may reach another device: no remote copies, remote signals or barrier semaphores. Data moves between devices by JAX's collectives and lax.ppermute only.
A program may use at most 64 MiB of HBM per device.

```python
import math
import jax
import jax.numpy as jnp
import numpy as np
from jax import lax

K = 16
F = 2048
ITERS = 2
NOBJ = 4096
NEP = 1024
NPIX = 128
MOST = 64
N_OBJ = 32


def draw_light_curves(key, part):
    key_strength = jax.random.fold_in(key, 101)
    key_amp = jax.random.fold_in(key, 102)
    key_mode = jax.random.fold_in(key, 103)
    key_noise = jax.random.fold_in(key, 104)
    key_jump = jax.random.fold_in(key, 105)
    key_size = jax.random.fold_in(key, 106)
    strength = jnp.exp(jax.random.uniform(key_strength, (K,), jnp.float32, math.log(0.3), math.log(3.0)))
    amplitude = jax.random.normal(key_amp, (NOBJ, K), jnp.float32) * strength[None, :]
    pattern = jax.random.normal(key_mode, (NEP, K), jnp.float32)
    trend = jnp.dot(amplitude, pattern.T, precision=lax.Precision.HIGHEST) * (1.5 / math.sqrt(K))
    noise = jax.random.normal(key_noise, (NOBJ, NEP), jnp.float32)
    jumps = jnp.where(jax.random.uniform(key_jump, (NOBJ, NEP), jnp.float32) < 0.02, 6.0 * jax.random.normal(key_size, (NOBJ, NEP), jnp.float32), 0.0)
    return jnp.clip(trend + noise + jumps, -40.0, 40.0).astype(jnp.float32)


def with_ends(drawn, rng, low, high):
    dims = drawn.shape
    spot = [jax.random.randint(jax.random.fold_in(rng, axis), (), 0, dims[axis]) for axis in range(len(dims))]
    drawn = drawn.at[tuple(spot)].set(low)
    longest = dims.index(max(dims))
    spot[longest] = (spot[longest] + 1) % dims[longest]
    return drawn.at[tuple(spot)].set(high)


def block_scale(own_key, dims, split, smallest, largest):
    loudness, own = 1.0, jax.random.fold_in(own_key, 6)
    for axis_at, blocks in split:
        steps = jnp.exp(jax.random.uniform(jax.random.fold_in(own, axis_at), (blocks,), jnp.float32, smallest / len(split), largest / len(split)))
        loudness = loudness * jnp.repeat(steps, dims[axis_at] // blocks).reshape([-1 if axis == axis_at else 1 for axis in range(len(dims))])
    return loudness


def split_up(amount, total, most, slope):
    loads = [(1 << 20) // math.isqrt(standing ** slope) + 1 for standing in range(2, amount + 1)]
    spare, holding = total - most - (amount - 1), [1] * (amount - 1)
    while spare > 0:
        candidates = [i for i in range(amount - 1) if holding[i] < most]
        mass, remaining = sum([loads[i] for i in candidates]), spare
        for i in candidates:
            extra = min(most - holding[i], max(1, remaining * loads[i] // mass), spare)
            holding[i] = holding[i] + extra
            spare = spare - extra
    return np.array([most] + holding)


def uneven(stream_key, amount, total, bound, lean):
    if amount == 2:
        one = jax.random.randint(stream_key, (), max(1, total - bound), min(bound, total - 1) + 1)
        return jnp.stack([one, total - one])
    lengths = jnp.asarray(split_up(amount, total, bound, lean), jnp.int32)
    twos = (amount - 1) // 2
    donor, receiver = lengths[1:1 + 2 * twos:2], lengths[2:2 + 2 * twos:2]
    margin = jnp.minimum(donor - 1, bound - receiver)
    shifted = jax.random.randint(jax.random.fold_in(stream_key, 1), (twos,), 0, 1 << 20) % (margin + 1)
    lengths = lengths.at[1:1 + 2 * twos:2].set(donor - shifted).at[2:2 + 2 * twos:2].set(receiver + shifted)
    return lengths[jax.random.permutation(jax.random.fold_in(stream_key, 2), amount)]


def bell_draw(rng, extent, deviation, most, cuts=(), held_as=jnp.bfloat16):
    factor_of = block_scale(rng, extent, cuts, -0.22, 0.18) if cuts else 1.0
    array = jax.random.normal(rng, extent, jnp.float32) * deviation * factor_of
    return jnp.minimum(jnp.maximum(array, -most), most).astype(held_as)


def setup_inputs(seed: int = 0) -> dict:
    key_of = jax.random.split(jax.random.key(seed), 8)
    return {
        "light_curves": draw_light_curves(jax.random.fold_in(key_of[7], 71), 0),
        "valid": with_ends((jax.random.randint(key_of[1], (NOBJ, NEP), 0, 4) < 3).astype(jnp.int32), jax.random.fold_in(key_of[1], 1), 0, 1),
        "pixel": jnp.searchsorted(jnp.cumsum(uneven(key_of[2], NPIX, NOBJ, MOST, 2)), jnp.arange(NOBJ), side="right").astype(jnp.int32),
        "inv_sigma": jnp.clip(jnp.exp(math.log(4.0) - 2.0794415 * jax.random.uniform(key_of[3], (NOBJ,), jnp.float32) ** block_scale(key_of[3], (NOBJ,), ((0, 32),), -0.2, 0.2)), 0.5, 4.0),
        "modes_init": bell_draw(key_of[4], (NEP, K), 1.0, 6.0, ((0, 8),), jnp.float32),
        "epoch_jitter": jnp.clip(jax.random.uniform(key_of[5], (NEP,), jnp.float32, 0.0, 0.9), 0.0, 0.9),
        "freq_index": with_ends(jax.random.randint(key_of[6], (F,), 4, 2 * NEP), jax.random.fold_in(key_of[6], 1), 4, (2 * NEP) - 1).astype(jnp.int32),
    }


HUBER = 1.345
DAMP = 2.0
RIDGE = 0.05
HIGHEST = lax.Precision.HIGHEST

def robust_weights(resid, mask_f, inv_sigma, pixel, npix):
    scaled = resid * inv_sigma[:, None]
    squares = lax.optimization_barrier(jnp.sum(mask_f * scaled * scaled, axis=1))
    valid_count = lax.optimization_barrier(jnp.sum(mask_f, axis=1))
    member = (pixel[None, :] == jnp.arange(npix, dtype=jnp.int32)[:, None]).astype(jnp.float32)
    sums = jnp.dot(member, squares, precision=HIGHEST)
    counts = jnp.dot(member, valid_count, precision=HIGHEST)
    spread = jnp.sqrt(sums / jnp.maximum(counts, 1.0) + 1e-06)
    object_spread = jnp.dot(spread, member, precision=HIGHEST)
    zscore = scaled / object_spread[:, None]
    huber = HUBER / jnp.maximum(jnp.abs(zscore), HUBER)
    return mask_f * huber * (inv_sigma * inv_sigma)[:, None]

def damped_solve(gram, target):
    order = target.shape[1]
    identity = jnp.eye(order, dtype=gram.dtype)
    return jnp.linalg.solve(gram + DAMP * identity, target[..., None])[..., 0]

def spectrum_sums(weighted, weight, times, freqs):
    cycles = times[:, None] * freqs[None, :]
    angle = 2.0 * math.pi * (cycles - jnp.floor(cycles))
    basis = jnp.concatenate([jnp.cos(angle), jnp.sin(angle), jnp.cos(2.0 * angle), jnp.sin(2.0 * angle)], axis=1).astype(jnp.bfloat16)
    width = freqs.shape[0]
    by_weight = jnp.dot(weight.astype(jnp.float32), basis.astype(jnp.float32), preferred_element_type=jnp.float32)
    by_value = jnp.dot(weighted.astype(jnp.float32), basis[:, :2 * width].astype(jnp.float32), preferred_element_type=jnp.float32)
    return (by_weight, by_value)

def powers(by_weight, by_value, total, level):
    width = by_value.shape[1] // 2
    cosine = by_weight[:, :width]
    sine = by_weight[:, width:2 * width]
    cosine_two = by_weight[:, 2 * width:3 * width]
    sine_two = by_weight[:, 3 * width:]
    mean_level = level / total
    ycos = by_value[:, :width] - mean_level * cosine
    ysin = by_value[:, width:] - mean_level * sine
    cc_term = 0.5 * (total + cosine_two) - cosine * cosine / total + RIDGE * total
    ss_term = 0.5 * (total - cosine_two) - sine * sine / total + RIDGE * total
    cs_term = 0.5 * sine_two - cosine * sine / total
    determinant = cc_term * ss_term - cs_term * cs_term
    return (ss_term * ycos * ycos + cc_term * ysin * ysin - 2.0 * cs_term * ycos * ysin) / determinant

def reference(light_curves, valid, pixel, inv_sigma, modes_init, epoch_jitter, freq_index):
    npix = 4 * N_OBJ
    mask_f = valid.astype(jnp.float32)
    modes = modes_init
    coef = jnp.zeros((NOBJ, K), jnp.float32)
    for iteration in range(ITERS):
        resid = light_curves - jnp.dot(coef, modes.T, precision=HIGHEST)
        weight = robust_weights(resid, mask_f, inv_sigma, pixel, npix)
        outer = (modes[:, :, None] * modes[:, None, :]).reshape(NEP, K * K)
        gram = jnp.dot(weight, outer, precision=HIGHEST).reshape(NOBJ, K, K)
        target = jnp.dot(weight * light_curves, modes, precision=HIGHEST)
        coef = damped_solve(gram, target)
        resid = light_curves - jnp.dot(coef, modes.T, precision=HIGHEST)
        weight = robust_weights(resid, mask_f, inv_sigma, pixel, npix)
        outer = (coef[:, :, None] * coef[:, None, :]).reshape(NOBJ, K * K)
        gram = jnp.dot(weight.T, outer, precision=HIGHEST).reshape(NEP, K, K)
        target = jnp.dot((weight * light_curves).T, coef, precision=HIGHEST)
        modes = damped_solve(gram, target)
    residual = light_curves - jnp.dot(coef, modes.T, precision=HIGHEST)
    final_weight = robust_weights(residual, mask_f, inv_sigma, pixel, npix)
    weighted = (final_weight * residual).astype(jnp.bfloat16)
    weight_b = final_weight.astype(jnp.bfloat16)
    total = lax.optimization_barrier(jnp.sum(weight_b, axis=1, keepdims=True, dtype=jnp.float32))
    level = lax.optimization_barrier(jnp.sum(weighted, axis=1, keepdims=True, dtype=jnp.float32))
    times = jnp.arange(NEP, dtype=jnp.int32).astype(jnp.float32) + epoch_jitter
    freqs = (freq_index + 1).astype(jnp.float32) / (4.0 * NEP)
    size = math.gcd(F, 512)
    blocks = freqs.reshape(F // size, size)

    def one_block(block_freqs):
        by_weight, by_value = spectrum_sums(weighted, weight_b, times, block_freqs)
        return powers(by_weight, by_value, total, level)
    power = lax.map(one_block, blocks)
    power = jnp.transpose(power, (1, 0, 2)).reshape(NOBJ, F)
    return (residual, power)
```

```python
import jax
import jax.numpy as jnp
import numpy as np
from jax import lax
from jax.experimental import pallas as pl
from jax.experimental.pallas import tpu as pltpu
from jax.sharding import PartitionSpec as P

ITERS = 2
HUBER = 1.345
DAMP = 2.0
RIDGE = 0.05
INVALID = 1e9
F32 = jnp.float32
BF16 = jnp.bfloat16
LANES = 128
VMEM = 48 << 20
NT = (((1,), (1,)), ((), ()))
NN = (((1,), (0,)), ((), ()))


def dot(a, b, dims):
    return lax.dot_general(a, b, dims, preferred_element_type=F32)


def split2(x):
    hi = x.astype(BF16)
    lo = (x - hi.astype(F32)).astype(BF16)
    return hi, lo


def split3(x):
    hi = x.astype(BF16).astype(F32)
    rest = x - hi
    mid = rest.astype(BF16).astype(F32)
    low = (rest - mid).astype(BF16).astype(F32)
    return hi, mid, low


def solve_columns(rows, target):
    order = len(rows)
    half = order // 2
    rows = list(rows)
    scaled = [None] * order
    forward = [None] * order
    for k in range(order):
        at = k if k < half else k - half
        row = rows[k]
        inverse = 1.0 / (row[at : at + 1] + DAMP)
        unit = row * inverse
        scaled[k] = unit
        value = target[k : k + 1] * inverse
        forward[k] = value
        for i in range(k + 1, order):
            here = i if k < half else i - half
            factor = row[here : here + 1]
            if i >= half and k < half:
                rows[i] = rows[i] - factor * unit[half:]
            else:
                rows[i] = rows[i] - factor * unit
        if k < half:
            target = target - row * value
        else:
            target = jnp.concatenate([target[:half], target[half:] - row * value], axis=0)
    width = target.shape[1]
    level = lax.broadcasted_iota(jnp.int32, (half, width), 0)
    upper = jnp.zeros((half, width), F32)
    lower = jnp.zeros((half, width), F32)
    for k in reversed(range(order)):
        unit = scaled[k]
        if k >= half:
            value = forward[k] - jnp.sum(unit * lower, axis=0, keepdims=True)
            lower = jnp.where(level == k - half, value, lower)
        else:
            both = unit[:half] * upper + unit[half:] * lower
            value = forward[k] - jnp.sum(both, axis=0, keepdims=True)
            upper = jnp.where(level == k, value, upper)
    return jnp.concatenate([upper, lower], axis=0)


def outer_rows(x):
    half = x.shape[0] // 2
    upper = [x[i : i + 1] * x for i in range(half)]
    lower = [x[i : i + 1] * x[half:] for i in range(half, 2 * half)]
    return jnp.concatenate(upper + lower, axis=0)


def rows_of(gram, order):
    half = order // 2
    top = [gram[order * i : order * (i + 1)] for i in range(half)]
    start = order * half
    return top + [gram[start + half * i : start + half * (i + 1)] for i in range(half)]


def coef_factors(coef_t):
    order = coef_t.shape[0]
    hi, mid, low = split3(coef_t)
    none = jnp.zeros((LANES - 6 * order, coef_t.shape[1]), F32)
    stack = jnp.concatenate([hi, mid, low, hi, mid, hi, none], axis=0)
    return stack.T.astype(BF16)


def mode_factors(modes_b):
    order = modes_b.shape[0]
    hi, mid, low = split3(modes_b)
    none = jnp.zeros((LANES - 6 * order, modes_b.shape[1]), F32)
    return jnp.concatenate([hi, hi, hi, mid, mid, low, none], axis=0).astype(BF16)


def window(meta):
    rows = meta.shape[1]
    filled = jnp.concatenate([meta, jnp.zeros((LANES - meta.shape[0], rows), F32)], axis=0)
    turned = filled.T
    same = (turned[:, 0:1] == meta[0:1]).astype(F32).astype(BF16)
    return same, turned[:, 1:2]


def block_of(win_ref, b, own_rows, order):
    coded = jnp.concatenate([win_ref[b, :own_rows], win_ref[b, own_rows + order :]], axis=0)
    ok = coded < 0.5 * INVALID
    return ok, jnp.where(ok, coded, 0.0)


def pixel_total(same, part):
    hi, mid, low = split3(part)
    wide = jnp.concatenate([hi, mid, low], axis=1).astype(BF16)
    total = dot(same, wide, NN)
    total = total[:, :LANES] + total[:, LANES : 2 * LANES] + total[:, 2 * LANES :]
    return jnp.sum(total, axis=1, keepdims=True)


def spread_of(same, part, count):
    return jnp.sqrt(pixel_total(same, part) / jnp.maximum(count, 1.0) + 1e-06)


def robust_weight(ok, scaled, edge, sigma):
    return jnp.where(ok, (sigma * sigma) * (edge / jnp.maximum(jnp.abs(scaled), edge)), 0.0)


def natural_modes(arrived, blocks, group, order):
    turns = LANES // group
    lane = lax.broadcasted_iota(jnp.int32, (order, LANES), 1)
    turned = arrived.T
    out = []
    for b in range(blocks):
        tile, inner = divmod(b * group, LANES)
        total = jnp.zeros((order, LANES), F32)
        for r in range(turns):
            piece = turned[order * r : order * (r + 1), LANES * tile : LANES * (tile + 1)]
            shift = (group * r - inner) % LANES
            if shift:
                piece = pltpu.roll(piece, shift, 1)
            inside = (lane >= group * r) & (lane < group * (r + 1))
            total = jnp.where(inside, piece, total)
        out.append(total)
    return out


def prep_kernel(lc_ref, valid_ref, pix_ref, sig_ref, init_ref, own_ref, tail_ref, head_ref):
    rows = lc_ref.shape[0]
    half = rows // 2
    coded = jnp.where(valid_ref[...] != 0, lc_ref[...], INVALID)
    own_ref[:rows] = coded
    own_ref[rows:] = init_ref[...]
    meta = jnp.concatenate(
        [pix_ref[...].astype(F32), sig_ref[...], jnp.zeros((6, rows), F32)], axis=0
    )
    tail_ref[:half] = coded[half:]
    tail_ref[half:] = meta
    head_ref[:half] = coded[:half]
    head_ref[half:] = meta


def widen_kernel(own_ref, left_ref, right_ref, pix_ref, sig_ref, out_ref, meta_ref):
    rows = pix_ref.shape[1]
    half = rows // 2
    own = own_ref[...]
    top = own.shape[0]
    left = left_ref[...]
    right = right_ref[...]
    for b in range(out_ref.shape[0]):
        out_ref[b, :top] = own
        out_ref[b, top : top + half] = left[:half]
        out_ref[b, top + half :] = right[:half]
    lane = lax.broadcasted_iota(jnp.int32, (8, rows), 1)
    beyond = pltpu.roll(jnp.where(lane >= half, left[half:], right[half:]), half, 1)
    meta_ref[:, :rows] = jnp.concatenate(
        [pix_ref[...].astype(F32), sig_ref[...], jnp.zeros((6, rows), F32)], axis=0
    )
    meta_ref[:, rows:] = beyond


def make_step_kernel(first):
    def kernel(*refs):
        if first:
            place_ref, meta_ref, win_ref = refs[:3]
            rest = refs[3:]
        else:
            place_ref, meta_ref, win_ref, arrived_ref, before_ref = refs[:5]
            rest = refs[5:]
        coef_ref, send_ref, scal_ref, wh_ref, wl_ref, ph_ref, pl_ref, oh_ref, ol_ref, mh_ref, ml_ref, ms_ref = rest
        blocks = win_ref.shape[0]
        order = coef_ref.shape[0]
        rows = meta_ref.shape[1]
        own_rows = rows // 2
        group = send_ref.shape[0] // 8
        same, sigma = window(meta_ref[...])
        if first:
            modes = [win_ref[b, own_rows : own_rows + order] for b in range(blocks)]
        else:
            modes = natural_modes(arrived_ref[...], blocks, group, order)
            factors = coef_factors(before_ref[...])
        part = jnp.zeros((rows, LANES), F32)
        seen = jnp.zeros((rows, LANES), F32)
        for b in range(blocks):
            ok, lc = block_of(win_ref, b, own_rows, order)
            ms_ref[b] = mode_factors(modes[b])
            if not first:
                lc = lc - dot(factors, ms_ref[b], NN)
            scaled = lc * sigma
            scal_ref[b] = scaled
            part = part + jnp.where(ok, scaled * scaled, 0.0)
            seen = seen + jnp.where(ok, 1.0, 0.0)
        count = jnp.sum(dot(same, seen.astype(BF16), NN), axis=1, keepdims=True)
        edge = HUBER * spread_of(same, part, count)
        for b in range(blocks):
            ok, lc = block_of(win_ref, b, own_rows, order)
            weight = robust_weight(ok, scal_ref[b], edge, sigma)
            at = slice(LANES * b, LANES * (b + 1))
            wh_ref[:, at], wl_ref[:, at] = split2(weight)
            ph_ref[:, at], pl_ref[:, at] = split2(weight * lc)
            oh_ref[:, at], ol_ref[:, at] = split2(outer_rows(modes[b]))
            mh_ref[:, at], ml_ref[:, at] = split2(modes[b])
        gram = (
            dot(oh_ref[...], wh_ref[...], NT)
            + dot(oh_ref[...], wl_ref[...], NT)
            + dot(ol_ref[...], wh_ref[...], NT)
        )
        target = (
            dot(mh_ref[...], ph_ref[...], NT)
            + dot(mh_ref[...], pl_ref[...], NT)
            + dot(ml_ref[...], ph_ref[...], NT)
        )
        coef_t = solve_columns(rows_of(gram, order), target)
        coef_ref[...] = coef_t
        factors = coef_factors(coef_t)
        part = jnp.zeros((rows, LANES), F32)
        for b in range(blocks):
            ok, lc = block_of(win_ref, b, own_rows, order)
            scaled = (lc - dot(factors, ms_ref[b], NN)) * sigma
            scal_ref[b] = scaled
            part = part + jnp.where(ok, scaled * scaled, 0.0)
        edge = HUBER * spread_of(same, part, count)
        place = place_ref[0]
        coded = win_ref[place, :own_rows]
        ok = coded < 0.5 * INVALID
        lc = jnp.where(ok, coded, 0.0)
        weight = robust_weight(ok, scal_ref[place, :own_rows], edge[:own_rows], sigma[:own_rows])
        weight_hi, weight_lo = split2(weight)
        value_hi, value_lo = split2(weight * lc)
        own_coef = coef_t[:, :own_rows]
        outer_hi, outer_lo = split2(outer_rows(own_coef))
        coef_hi, coef_lo = split2(own_coef)
        gram = dot(outer_hi, weight_hi, NN) + dot(outer_hi, weight_lo, NN) + dot(outer_lo, weight_hi, NN)
        target = dot(coef_hi, value_hi, NN) + dot(coef_hi, value_lo, NN) + dot(coef_lo, value_hi, NN)
        spare = jnp.zeros((2 * LANES - gram.shape[0] - order, LANES), F32)
        tall = jnp.concatenate([gram, target, spare], axis=0)
        turns = LANES // group
        for side in range(2):
            turned = tall[LANES * side : LANES * (side + 1)].T
            for r in range(turns):
                send_ref[pl.ds(turns * side + r, group, stride=8), :] = turned[group * r : group * (r + 1)]

    return kernel


def mode_kernel(arrived_ref, out_ref, *, order):
    total = arrived_ref[0]
    for j in range(1, arrived_ref.shape[0]):
        total = total + arrived_ref[j]
    turns = total.shape[0] // 2
    tall = jnp.concatenate([total, jnp.zeros((LANES - 2 * turns, LANES), F32)], axis=0).T
    after = pltpu.roll(tall, LANES - turns, 1)
    half = order // 2
    gram = jnp.concatenate([tall, after[: half * half]], axis=0)
    target = after[half * half : half * half + order]
    solved = solve_columns(rows_of(gram, order), target)
    lane = lax.broadcasted_iota(jnp.int32, solved.shape, 1)
    solved = jnp.where(lane < turns, solved, 0.0)
    wide = jnp.concatenate([solved, jnp.zeros((LANES - order, LANES), F32)], axis=0).T
    line = wide[0:1]
    for r in range(1, turns):
        line = line + pltpu.roll(wide[0:8], order * r, 1)[r : r + 1]
    out_ref[...] = jnp.broadcast_to(line.reshape(1, 1, LANES), out_ref.shape)


def sine_series(terms):
    x = (np.cos(np.pi * (np.arange(400) + 0.5) / 400) + 1) / 2 * 0.0625
    v = np.sqrt(x)
    scale = 0.0625
    grid = x / scale
    sine = np.polynomial.polynomial.polyfit(grid, np.sin(2 * np.pi * v) / v, terms)
    cosine = np.polynomial.polynomial.polyfit(grid, np.cos(2 * np.pi * v), terms)
    power = scale ** np.arange(terms + 1)
    return [float(c) for c in sine / power], [float(c) for c in cosine / power]


SINE, COSINE = sine_series(6)


def horner(series, x):
    total = jnp.full(x.shape, series[-1], F32)
    for c in series[-2::-1]:
        total = total * x + c
    return total


def basis_kernel(jitter_ref, freq_ref, out_ref):
    blocks, width = jitter_ref.shape[0], freq_ref.shape[1]
    jitter = jnp.concatenate([jitter_ref[...], jnp.zeros((LANES - blocks, LANES), F32)], axis=0).T
    freqs = freq_ref[...]
    for b in range(blocks):
        index = lax.broadcasted_iota(jnp.int32, (LANES, 1), 0) + LANES * b
        times = index.astype(F32) + jitter[:, b : b + 1]
        cycles = times * freqs
        turn = cycles - jnp.floor(cycles)
        turn = jnp.where(turn >= 0.5, turn - 1.0, turn)
        far = jnp.abs(turn) > 0.25
        near = jnp.where(far, jnp.where(turn > 0.0, 0.5, -0.5) - turn, turn)
        square = near * near
        sine = near * horner(SINE, square)
        cosine = horner(COSINE, square)
        cosine = jnp.where(far, -cosine, cosine)
        at = slice(LANES * b, LANES * (b + 1))
        out_ref[at, :width] = cosine.astype(BF16)
        out_ref[at, width : 2 * width] = sine.astype(BF16)
        out_ref[at, 2 * width : 3 * width] = (1.0 - 2.0 * sine * sine).astype(BF16)
        out_ref[at, 3 * width :] = (2.0 * sine * cosine).astype(BF16)


def final_kernel(place_ref, meta_ref, win_ref, arrived_ref, coef_ref, basis_ref, lc_ref,
                 resid_ref, power_ref, res_ref, w_ref, q_ref, *, group):
    blocks = win_ref.shape[0]
    order = coef_ref.shape[0]
    rows = meta_ref.shape[1]
    own_rows = rows // 2
    same, sigma = window(meta_ref[...])
    modes = natural_modes(arrived_ref[...], blocks, group, order)
    factors = coef_factors(coef_ref[...])
    part = jnp.zeros((rows, LANES), F32)
    seen = jnp.zeros((rows, LANES), F32)
    for b in range(blocks):
        ok, lc = block_of(win_ref, b, own_rows, order)
        trend = dot(factors, mode_factors(modes[b]), NN)
        resid = lc - trend
        res_ref[b] = resid[:own_rows]
        scaled = resid * sigma
        part = part + jnp.where(ok, scaled * scaled, 0.0)
        seen = seen + jnp.where(ok, 1.0, 0.0)
    count = jnp.sum(dot(same, seen.astype(BF16), NN), axis=1, keepdims=True)
    edge = (HUBER * spread_of(same, part, count))[:own_rows]
    sigma = sigma[:own_rows]
    total = jnp.zeros((own_rows, LANES), F32)
    level = jnp.zeros((own_rows, LANES), F32)
    for b in range(blocks):
        ok = win_ref[b, :own_rows] < 0.5 * INVALID
        resid = res_ref[b]
        weight = robust_weight(ok, resid * sigma, edge, sigma)
        at = slice(LANES * b, LANES * (b + 1))
        weight_b = weight.astype(BF16)
        value_b = (weight * resid).astype(BF16)
        w_ref[:, at] = weight_b
        q_ref[:, at] = value_b
        total = total + weight_b.astype(F32)
        level = level + value_b.astype(F32)
    place = place_ref[0]
    resid = res_ref[place]
    ok = win_ref[place, :own_rows] < 0.5 * INVALID
    resid_ref[...] = jnp.where(ok, resid, lc_ref[...] + resid)
    total = jnp.sum(total, axis=1, keepdims=True)
    level = jnp.sum(level, axis=1, keepdims=True)
    by_weight = dot(w_ref[...], basis_ref[...], NN)
    width = by_weight.shape[1] // 4
    by_value = dot(q_ref[...], basis_ref[:, : 2 * width], NN)
    cosine = by_weight[:, :width]
    sine = by_weight[:, width : 2 * width]
    cosine_two = by_weight[:, 2 * width : 3 * width]
    sine_two = by_weight[:, 3 * width :]
    inverse = 1.0 / total
    mean_level = level * inverse
    ycos = by_value[:, :width] - mean_level * cosine
    ysin = by_value[:, width:] - mean_level * sine
    cc_term = 0.5 * (total + cosine_two) - cosine * cosine * inverse + RIDGE * total
    ss_term = 0.5 * (total - cosine_two) - sine * sine * inverse + RIDGE * total
    cs_term = 0.5 * sine_two - cosine * sine * inverse
    determinant = cc_term * ss_term - cs_term * cs_term
    power = (ss_term * ycos * ycos + cc_term * ysin * ysin - 2.0 * cs_term * ycos * ysin) / determinant
    power_ref[...] = power.astype(BF16)


def place_kernel(in_ref, out_ref):
    width = in_ref.shape[2]
    for b in range(in_ref.shape[0]):
        out_ref[:, width * b : width * (b + 1)] = in_ref[b].astype(F32)


def shaped(shape, dtype=F32):
    return jax.ShapeDtypeStruct(shape, dtype)


def call(kernel, out_shape, args, scratch=(), scalar=False, staged=(), name=None):
    specs = [
        pl.BlockSpec(a.shape, lambda i, n=a.ndim: (0,) * n)
        if at in staged
        else pl.BlockSpec(memory_space=pltpu.VMEM)
        for at, a in enumerate(args)
    ]
    if scalar:
        specs[0] = pl.BlockSpec(memory_space=pltpu.SMEM)
    many = isinstance(out_shape, (tuple, list))
    out_specs = [pl.BlockSpec(memory_space=pltpu.VMEM) for _ in (out_shape if many else [0])]
    return pl.pallas_call(
        kernel,
        grid=(1,),
        out_shape=out_shape,
        in_specs=specs,
        out_specs=out_specs if many else out_specs[0],
        scratch_shapes=list(scratch),
        compiler_params=pltpu.CompilerParams(vmem_limit_bytes=VMEM),
        name=name,
    )(*args)


def per_device(light_curves, valid, pixel, inv_sigma, modes_init, epoch_jitter, freq_index):
    obj_count = lax.axis_size("obj")
    ep_count = lax.axis_size("ep")
    rows, cols = light_curves.shape
    order = modes_init.shape[1]
    half = rows // 2
    span = ep_count * cols
    group = obj_count
    place = lax.axis_index("ep").astype(jnp.int32)
    places = place.reshape(1)

    pixels = pixel.reshape(1, rows)
    sigmas = inv_sigma.reshape(1, rows)
    own, tail, head = call(
        prep_kernel,
        (shaped((rows + order, cols)), shaped((half + 8, cols)), shaped((half + 8, cols))),
        (light_curves, valid, pixels, sigmas, modes_init.T),
        staged=range(5),
        name="prep",
    )
    ring = [(i, (i + 1) % obj_count) for i in range(obj_count)]
    back = [(i, (i - 1) % obj_count) for i in range(obj_count)]
    left = lax.ppermute(tail, "obj", ring)
    right = lax.ppermute(head, "obj", back)
    wide, meta = call(
        widen_kernel,
        (shaped((ep_count, 2 * rows + order, cols)), shaped((8, 2 * rows))),
        (own, left, right, pixels, sigmas),
        staged=(3, 4),
        name="widen",
    )
    win = lax.all_to_all(wide, "ep", split_axis=0, concat_axis=0, tiled=True)

    width = freq_index.shape[0] // ep_count
    freqs = (lax.dynamic_slice_in_dim(freq_index, place * width, width) + 1).astype(F32) / (4.0 * span)
    basis = call(
        basis_kernel,
        shaped((span, 4 * width), BF16),
        (epoch_jitter.reshape(ep_count, cols), freqs.reshape(1, width)),
        name="basis",
    )

    window_rows = 2 * rows
    products = order * order * 3 // 4
    scratch = [
        pltpu.VMEM((ep_count, window_rows, LANES), F32),
        pltpu.VMEM((window_rows, span), BF16),
        pltpu.VMEM((window_rows, span), BF16),
        pltpu.VMEM((window_rows, span), BF16),
        pltpu.VMEM((window_rows, span), BF16),
        pltpu.VMEM((products, span), BF16),
        pltpu.VMEM((products, span), BF16),
        pltpu.VMEM((order, span), BF16),
        pltpu.VMEM((order, span), BF16),
        pltpu.VMEM((ep_count, LANES, LANES), BF16),
    ]
    args = (places, meta, win)
    everyone = ep_count * obj_count
    for iteration in range(ITERS):
        coef_t, send = call(
            make_step_kernel(iteration == 0),
            (shaped((order, window_rows)), shaped((8 * group, LANES))),
            args,
            scratch=scratch,
            scalar=True,
            name=f"objects_{iteration}",
        )
        arrived = lax.all_to_all(
            send.reshape(group, 8, LANES), "obj", split_axis=0, concat_axis=0, tiled=True
        )
        lines = call(
            lambda a, o: mode_kernel(a, o, order=order),
            shaped((everyone, 1, LANES)),
            (arrived,),
            name=f"modes_{iteration}",
        )
        lines = lax.all_to_all(lines, ("ep", "obj"), split_axis=0, concat_axis=0, tiled=True)
        args = (places, meta, win, lines.reshape(everyone, LANES), coef_t)
    residual, power = call(
        lambda *refs: final_kernel(*refs, group=group),
        (shaped((rows, cols)), shaped((rows, width), BF16)),
        (*args, basis, light_curves),
        staged=(6,),
        scratch=[
            pltpu.VMEM((ep_count, rows, LANES), F32),
            pltpu.VMEM((rows, span), BF16),
            pltpu.VMEM((rows, span), BF16),
        ],
        scalar=True,
        name="spectrum",
    )
    share = rows // ep_count
    power = lax.all_to_all(
        power.reshape(ep_count, share, width), "ep", split_axis=0, concat_axis=0, tiled=True
    )
    power = call(place_kernel, shaped((share, ep_count * width)), (power,), name="place")
    return residual, power


def solution(mesh):
    in_specs = (P("obj", "ep"), P("obj", "ep"), P("obj"), P("obj"), P("ep", None), P(), P())
    out_specs = (P("obj", "ep"), P(("obj", "ep"), None))
    return jax.shard_map(
        per_device, mesh=mesh, in_specs=in_specs, out_specs=out_specs, check_vma=False
    )
```

```python
import jax
import jax.numpy as jnp
import numpy as np
from jax import lax
from jax.experimental import pallas as pl
from jax.experimental.pallas import tpu as pltpu
from jax.sharding import PartitionSpec as P

ITERS = 2
HUBER = 1.345
DAMP = 2.0
RIDGE = 0.05
INVALID = 1e9
F32 = jnp.float32
BF16 = jnp.bfloat16
LANES = 128
VMEM = 14 << 20
NT = (((1,), (1,)), ((), ()))
NN = (((1,), (0,)), ((), ()))


def dot(a, b, dims):
    return lax.dot_general(a, b, dims, preferred_element_type=F32)


def split2(x):
    hi = x.astype(BF16)
    lo = (x - hi.astype(F32)).astype(BF16)
    return hi, lo


def split3(x):
    hi = x.astype(BF16).astype(F32)
    rest = x - hi
    mid = rest.astype(BF16).astype(F32)
    low = (rest - mid).astype(BF16).astype(F32)
    return hi, mid, low


def solve_columns(rows, target):
    order = len(rows)
    half = order // 2
    rows = list(rows)
    scaled = [None] * order
    forward = [None] * order
    for k in range(order):
        at = k if k < half else k - half
        row = rows[k]
        inverse = 1.0 / (row[at : at + 1] + DAMP)
        unit = row * inverse
        scaled[k] = unit
        value = target[k : k + 1] * inverse
        forward[k] = value
        for i in range(k + 1, order):
            here = i if k < half else i - half
            factor = row[here : here + 1]
            if i >= half and k < half:
                rows[i] = rows[i] - factor * unit[half:]
            else:
                rows[i] = rows[i] - factor * unit
        if k < half:
            target = target - row * value
        else:
            target = jnp.concatenate([target[:half], target[half:] - row * value], axis=0)
    width = target.shape[1]
    level = lax.broadcasted_iota(jnp.int32, (half, width), 0)
    upper = jnp.zeros((half, width), F32)
    lower = jnp.zeros((half, width), F32)
    for k in reversed(range(order)):
        unit = scaled[k]
        if k >= half:
            value = forward[k] - jnp.sum(unit * lower, axis=0, keepdims=True)
            lower = jnp.where(level == k - half, value, lower)
        else:
            both = unit[:half] * upper + unit[half:] * lower
            value = forward[k] - jnp.sum(both, axis=0, keepdims=True)
            upper = jnp.where(level == k, value, upper)
    return jnp.concatenate([upper, lower], axis=0)


def outer_rows(x):
    half = x.shape[0] // 2
    upper = [x[i : i + 1] * x for i in range(half)]
    lower = [x[i : i + 1] * x[half:] for i in range(half, 2 * half)]
    return jnp.concatenate(upper + lower, axis=0)


def rows_of(gram, order):
    half = order // 2
    top = [gram[order * i : order * (i + 1)] for i in range(half)]
    start = order * half
    return top + [gram[start + half * i : start + half * (i + 1)] for i in range(half)]


def coef_factors(coef_t):
    order = coef_t.shape[0]
    hi, mid, low = split3(coef_t)
    none = jnp.zeros((LANES - 6 * order, coef_t.shape[1]), F32)
    stack = jnp.concatenate([hi, mid, low, hi, mid, hi, none], axis=0)
    return stack.T.astype(BF16)


def mode_factors(modes_b):
    order = modes_b.shape[0]
    hi, mid, low = split3(modes_b)
    none = jnp.zeros((LANES - 6 * order, modes_b.shape[1]), F32)
    return jnp.concatenate([hi, hi, hi, mid, mid, low, none], axis=0).astype(BF16)


def window(meta):
    rows = meta.shape[1]
    filled = jnp.concatenate([meta, jnp.zeros((LANES - meta.shape[0], rows), F32)], axis=0)
    turned = filled.T
    same = (turned[:, 0:1] == meta[0:1]).astype(F32).astype(BF16)
    return same, turned[:, 1:2]


def block_of(win_ref, b, own_rows, order):
    coded = jnp.concatenate([win_ref[b, :own_rows], win_ref[b, own_rows + order :]], axis=0)
    ok = coded < 0.5 * INVALID
    return ok, jnp.where(ok, coded, 0.0)


def pixel_total(same, part):
    hi, mid, low = split3(part)
    wide = jnp.concatenate([hi, mid, low], axis=1).astype(BF16)
    total = dot(same, wide, NN)
    total = total[:, :LANES] + total[:, LANES : 2 * LANES] + total[:, 2 * LANES :]
    return jnp.sum(total, axis=1, keepdims=True)


def spread_of(same, part, count):
    return jnp.sqrt(pixel_total(same, part) / jnp.maximum(count, 1.0) + 1e-06)


def robust_weight(ok, scaled, edge, sigma):
    return jnp.where(ok, (sigma * sigma) * (edge / jnp.maximum(jnp.abs(scaled), edge)), 0.0)


def natural_modes(arrived, blocks, group, order):
    turns = LANES // group
    lane = lax.broadcasted_iota(jnp.int32, (order, LANES), 1)
    turned = arrived.T
    out = []
    for b in range(blocks):
        tile, inner = divmod(b * group, LANES)
        total = jnp.zeros((order, LANES), F32)
        for r in range(turns):
            piece = turned[order * r : order * (r + 1), LANES * tile : LANES * (tile + 1)]
            shift = (group * r - inner) % LANES
            if shift:
                piece = pltpu.roll(piece, shift, 1)
            inside = (lane >= group * r) & (lane < group * (r + 1))
            total = jnp.where(inside, piece, total)
        out.append(total)
    return out


def prep_kernel(lc_hbm, valid_hbm, pix_hbm, sig_hbm, init_hbm, own_ref, tail_ref, head_ref,
                lc_ref, valid_ref, pix_ref, sig_ref, init_ref, sems):
    pairs = (
        (lc_hbm, lc_ref), (valid_hbm, valid_ref), (pix_hbm, pix_ref), (sig_hbm, sig_ref), (init_hbm, init_ref)
    )
    copies = [pltpu.make_async_copy(a, b, sems.at[i]) for i, (a, b) in enumerate(pairs)]
    for copy in copies:
        copy.start()
    for copy in copies:
        copy.wait()
    rows = lc_ref.shape[0]
    half = rows // 2
    coded = jnp.where(valid_ref[...] != 0, lc_ref[...], INVALID)
    own_ref[:rows] = coded
    own_ref[rows:] = init_ref[...]
    meta = jnp.concatenate(
        [pix_ref[...].astype(F32), sig_ref[...], jnp.zeros((6, rows), F32)], axis=0
    )
    tail_ref[:half] = coded[half:]
    tail_ref[half:] = meta
    head_ref[:half] = coded[:half]
    head_ref[half:] = meta


def widen_kernel(own_ref, tail_ref, left_ref, right_ref, out_ref, meta_ref):
    rows = tail_ref.shape[1]
    half = rows // 2
    own = own_ref[...]
    top = own.shape[0]
    left = left_ref[...]
    right = right_ref[...]
    for b in range(out_ref.shape[0]):
        out_ref[b, :top] = own
        out_ref[b, top : top + half] = left[:half]
        out_ref[b, top + half :] = right[:half]
    lane = lax.broadcasted_iota(jnp.int32, (8, rows), 1)
    beyond = pltpu.roll(jnp.where(lane >= half, left[half:], right[half:]), half, 1)
    meta_ref[:, :rows] = tail_ref[half:]
    meta_ref[:, rows:] = beyond


def make_step_kernel(first):
    def kernel(*refs):
        if first:
            place_ref, meta_ref, win_ref = refs[:3]
            rest = refs[3:]
        else:
            place_ref, meta_ref, win_ref, arrived_ref, before_ref = refs[:5]
            rest = refs[5:]
        coef_ref, send_ref, scal_ref, wh_ref, wl_ref, ph_ref, pl_ref, oh_ref, ol_ref, mh_ref, ml_ref, ms_ref = rest
        blocks = win_ref.shape[0]
        order = coef_ref.shape[0]
        rows = meta_ref.shape[1]
        own_rows = rows // 2
        group = send_ref.shape[0] // 8
        same, sigma = window(meta_ref[...])
        if first:
            modes = [win_ref[b, own_rows : own_rows + order] for b in range(blocks)]
        else:
            modes = natural_modes(arrived_ref[...], blocks, group, order)
            factors = coef_factors(before_ref[...])
        part = jnp.zeros((rows, LANES), F32)
        seen = jnp.zeros((rows, LANES), F32)
        for b in range(blocks):
            ok, lc = block_of(win_ref, b, own_rows, order)
            ms_ref[b] = mode_factors(modes[b])
            if not first:
                lc = lc - dot(factors, ms_ref[b], NN)
            scaled = lc * sigma
            scal_ref[b] = scaled
            part = part + jnp.where(ok, scaled * scaled, 0.0)
            seen = seen + jnp.where(ok, 1.0, 0.0)
        count = jnp.sum(dot(same, seen.astype(BF16), NN), axis=1, keepdims=True)
        edge = HUBER * spread_of(same, part, count)
        for b in range(blocks):
            ok, lc = block_of(win_ref, b, own_rows, order)
            weight = robust_weight(ok, scal_ref[b], edge, sigma)
            at = slice(LANES * b, LANES * (b + 1))
            wh_ref[:, at], wl_ref[:, at] = split2(weight)
            ph_ref[:, at], pl_ref[:, at] = split2(weight * lc)
            oh_ref[:, at], ol_ref[:, at] = split2(outer_rows(modes[b]))
            mh_ref[:, at], ml_ref[:, at] = split2(modes[b])
        gram = (
            dot(oh_ref[...], wh_ref[...], NT)
            + dot(oh_ref[...], wl_ref[...], NT)
            + dot(ol_ref[...], wh_ref[...], NT)
        )
        target = (
            dot(mh_ref[...], ph_ref[...], NT)
            + dot(mh_ref[...], pl_ref[...], NT)
            + dot(ml_ref[...], ph_ref[...], NT)
        )
        coef_t = solve_columns(rows_of(gram, order), target)
        coef_ref[...] = coef_t
        factors = coef_factors(coef_t)
        part = jnp.zeros((rows, LANES), F32)
        for b in range(blocks):
            ok, lc = block_of(win_ref, b, own_rows, order)
            scaled = (lc - dot(factors, ms_ref[b], NN)) * sigma
            scal_ref[b] = scaled
            part = part + jnp.where(ok, scaled * scaled, 0.0)
        edge = HUBER * spread_of(same, part, count)
        place = place_ref[0]
        coded = win_ref[place, :own_rows]
        ok = coded < 0.5 * INVALID
        lc = jnp.where(ok, coded, 0.0)
        weight = robust_weight(ok, scal_ref[place, :own_rows], edge[:own_rows], sigma[:own_rows])
        weight_hi, weight_lo = split2(weight)
        value_hi, value_lo = split2(weight * lc)
        own_coef = coef_t[:, :own_rows]
        outer_hi, outer_lo = split2(outer_rows(own_coef))
        coef_hi, coef_lo = split2(own_coef)
        gram = dot(outer_hi, weight_hi, NN) + dot(outer_hi, weight_lo, NN) + dot(outer_lo, weight_hi, NN)
        target = dot(coef_hi, value_hi, NN) + dot(coef_hi, value_lo, NN) + dot(coef_lo, value_hi, NN)
        spare = jnp.zeros((2 * LANES - gram.shape[0] - order, LANES), F32)
        tall = jnp.concatenate([gram, target, spare], axis=0)
        turns = LANES // group
        for side in range(2):
            turned = tall[LANES * side : LANES * (side + 1)].T
            for r in range(turns):
                send_ref[pl.ds(turns * side + r, group, stride=8), :] = turned[group * r : group * (r + 1)]

    return kernel


def mode_kernel(arrived_ref, out_ref, *, order):
    total = arrived_ref[0]
    for j in range(1, arrived_ref.shape[0]):
        total = total + arrived_ref[j]
    turns = total.shape[0] // 2
    tall = jnp.concatenate([total, jnp.zeros((LANES - 2 * turns, LANES), F32)], axis=0).T
    after = pltpu.roll(tall, LANES - turns, 1)
    half = order // 2
    gram = jnp.concatenate([tall, after[: half * half]], axis=0)
    target = after[half * half : half * half + order]
    solved = solve_columns(rows_of(gram, order), target)
    lane = lax.broadcasted_iota(jnp.int32, solved.shape, 1)
    solved = jnp.where(lane < turns, solved, 0.0)
    wide = jnp.concatenate([solved, jnp.zeros((LANES - order, LANES), F32)], axis=0).T
    line = wide[0:1]
    for r in range(1, turns):
        line = line + pltpu.roll(wide[0:8], order * r, 1)[r : r + 1]
    out_ref[...] = jnp.broadcast_to(line.reshape(1, 1, LANES), out_ref.shape)


def half_turn_series():
    grid = (np.cos(np.pi * (np.arange(400) + 0.5) / 400) + 1) / 2
    u = np.sqrt(grid) / 2
    sine = np.polynomial.polynomial.polyfit(grid, np.sin(np.pi * u) / u, 5)
    cosine = np.polynomial.polynomial.polyfit(grid, np.cos(np.pi * u), 5)
    power = 0.25 ** np.arange(6)
    return [float(c) for c in sine / power], [float(c) for c in cosine / power]


SINE, COSINE = half_turn_series()


def horner(series, x):
    total = x * series[-1] + series[-2]
    for c in series[-3::-1]:
        total = total * x + c
    return total


def basis_kernel(jitter_ref, freq_ref, out_ref, time_ref):
    blocks, width = jitter_ref.shape[0], freq_ref.shape[1]
    jitter = jnp.concatenate([jitter_ref[...], jnp.zeros((LANES - blocks, LANES), F32)], axis=0).T
    index = lax.broadcasted_iota(jnp.int32, (LANES, LANES), 0)
    for b in range(blocks):
        time_ref[LANES * b : LANES * (b + 1)] = (index + LANES * b).astype(F32) + jitter[:, b : b + 1]
    step = 32

    @pl.loop(0, time_ref.shape[0] // step)
    def _(i):
        at = pl.ds(pl.multiple_of(step * i, step), step)
        times = time_ref[at]
        for c in range(width // LANES):
            cycles = times * freq_ref[:, LANES * c : LANES * (c + 1)]
            turn = cycles - jnp.floor(cycles + 0.5)
            square = turn * turn
            sine = turn * horner(SINE, square)
            cosine = horner(COSINE, square)
            for k in range(2):
                twice = sine + sine
                sine, cosine = twice * cosine, 1.0 - twice * sine
                start = 2 * k * width + LANES * c
                out_ref[at, start : start + LANES] = cosine.astype(BF16)
                out_ref[at, start + width : start + width + LANES] = sine.astype(BF16)


def final_kernel(place_ref, meta_ref, win_ref, arrived_ref, coef_ref, basis_ref, lc_ref,
                 resid_ref, power_ref, res_ref, w_ref, q_ref, *, group):
    blocks = win_ref.shape[0]
    order = coef_ref.shape[0]
    rows = meta_ref.shape[1]
    own_rows = rows // 2
    same, sigma = window(meta_ref[...])
    modes = natural_modes(arrived_ref[...], blocks, group, order)
    factors = coef_factors(coef_ref[...])
    part = jnp.zeros((rows, LANES), F32)
    seen = jnp.zeros((rows, LANES), F32)
    for b in range(blocks):
        ok, lc = block_of(win_ref, b, own_rows, order)
        trend = dot(factors, mode_factors(modes[b]), NN)
        resid = lc - trend
        res_ref[b] = resid[:own_rows]
        scaled = resid * sigma
        part = part + jnp.where(ok, scaled * scaled, 0.0)
        seen = seen + jnp.where(ok, 1.0, 0.0)
    count = jnp.sum(dot(same, seen.astype(BF16), NN), axis=1, keepdims=True)
    edge = (HUBER * spread_of(same, part, count))[:own_rows]
    sigma = sigma[:own_rows]
    total = jnp.zeros((own_rows, LANES), F32)
    level = jnp.zeros((own_rows, LANES), F32)
    for b in range(blocks):
        ok = win_ref[b, :own_rows] < 0.5 * INVALID
        resid = res_ref[b]
        weight = robust_weight(ok, resid * sigma, edge, sigma)
        at = slice(LANES * b, LANES * (b + 1))
        weight_b = weight.astype(BF16)
        value_b = (weight * resid).astype(BF16)
        w_ref[:, at] = weight_b
        q_ref[:, at] = value_b
        total = total + weight_b.astype(F32)
        level = level + value_b.astype(F32)
    place = place_ref[0]
    resid = res_ref[place]
    ok = win_ref[place, :own_rows] < 0.5 * INVALID
    resid_ref[...] = jnp.where(ok, resid, lc_ref[...] + resid)
    total = jnp.sum(total, axis=1, keepdims=True)
    level = jnp.sum(level, axis=1, keepdims=True)
    by_weight = dot(w_ref[...], basis_ref[...], NN)
    width = by_weight.shape[1] // 4
    by_value = dot(q_ref[...], basis_ref[:, : 2 * width], NN)
    cosine = by_weight[:, :width]
    sine = by_weight[:, width : 2 * width]
    cosine_two = by_weight[:, 2 * width : 3 * width]
    sine_two = by_weight[:, 3 * width :]
    inverse = 1.0 / total
    mean_level = level * inverse
    ycos = by_value[:, :width] - mean_level * cosine
    ysin = by_value[:, width:] - mean_level * sine
    cc_term = 0.5 * (total + cosine_two) - cosine * cosine * inverse + RIDGE * total
    ss_term = 0.5 * (total - cosine_two) - sine * sine * inverse + RIDGE * total
    cs_term = 0.5 * sine_two - cosine * sine * inverse
    determinant = cc_term * ss_term - cs_term * cs_term
    power = (ss_term * ycos * ycos + cc_term * ysin * ysin - 2.0 * cs_term * ycos * ysin) / determinant
    power_ref[...] = power.astype(BF16)


def place_kernel(in_ref, out_ref):
    width = in_ref.shape[2]
    for b in range(in_ref.shape[0]):
        out_ref[:, width * b : width * (b + 1)] = in_ref[b].astype(F32)


def shaped(shape, dtype=F32):
    return jax.ShapeDtypeStruct(shape, dtype)


def call(kernel, out_shape, args, scratch=(), scalar=False, away=(), out_space=pltpu.VMEM, limit=VMEM, name=None):
    specs = [pl.BlockSpec(memory_space=pltpu.HBM if at in away else pltpu.VMEM) for at in range(len(args))]
    if scalar:
        specs[0] = pl.BlockSpec(memory_space=pltpu.SMEM)
    many = isinstance(out_shape, (tuple, list))
    out_specs = [pl.BlockSpec(memory_space=out_space) for _ in (out_shape if many else [0])]
    return pl.pallas_call(
        kernel,
        out_shape=out_shape,
        in_specs=specs,
        out_specs=out_specs if many else out_specs[0],
        scratch_shapes=list(scratch),
        compiler_params=pltpu.CompilerParams(vmem_limit_bytes=limit),
        name=name,
    )(*args)


def per_device(light_curves, valid, pixel, inv_sigma, modes_init, epoch_jitter, freq_index):
    obj_count = lax.axis_size("obj")
    ep_count = lax.axis_size("ep")
    rows, cols = light_curves.shape
    order = modes_init.shape[1]
    half = rows // 2
    span = ep_count * cols
    group = obj_count
    place = lax.axis_index("ep").astype(jnp.int32)
    places = place.reshape(1)

    fetched = (light_curves, valid, pixel.reshape(1, rows), inv_sigma.reshape(1, rows), modes_init.T)
    fetched = tuple(pltpu.with_memory_space_constraint(a, pltpu.HBM) for a in fetched)
    own, tail, head = call(
        prep_kernel,
        (shaped((rows + order, cols)), shaped((half + 8, cols)), shaped((half + 8, cols))),
        fetched,
        scratch=[pltpu.VMEM(a.shape, a.dtype) for a in fetched] + [pltpu.SemaphoreType.DMA((5,))],
        away=range(5),
        name="prep",
    )
    ring = [(i, (i + 1) % obj_count) for i in range(obj_count)]
    back = [(i, (i - 1) % obj_count) for i in range(obj_count)]
    left = lax.ppermute(tail, "obj", ring)
    right = lax.ppermute(head, "obj", back)
    wide, meta = call(
        widen_kernel,
        (shaped((ep_count, 2 * rows + order, cols)), shaped((8, 2 * rows))),
        (own, tail, left, right),
        name="widen",
    )
    width = freq_index.shape[0] // ep_count
    freqs = (lax.dynamic_slice_in_dim(freq_index, place * width, width) + 1).astype(F32) / (4.0 * span)
    wide, freqs = lax.optimization_barrier((wide, freqs))
    win = lax.all_to_all(wide, "ep", split_axis=0, concat_axis=0, tiled=True)
    basis = call(
        basis_kernel,
        shaped((span, 4 * width), BF16),
        (epoch_jitter.reshape(ep_count, cols), freqs.reshape(1, width)),
        scratch=[pltpu.VMEM((span, LANES), F32)],
        name="basis",
    )
    win, basis = lax.optimization_barrier((win, basis))

    window_rows = 2 * rows
    products = order * order * 3 // 4
    scratch = [
        pltpu.VMEM((ep_count, window_rows, LANES), F32),
        pltpu.VMEM((window_rows, span), BF16),
        pltpu.VMEM((window_rows, span), BF16),
        pltpu.VMEM((window_rows, span), BF16),
        pltpu.VMEM((window_rows, span), BF16),
        pltpu.VMEM((products, span), BF16),
        pltpu.VMEM((products, span), BF16),
        pltpu.VMEM((order, span), BF16),
        pltpu.VMEM((order, span), BF16),
        pltpu.VMEM((ep_count, LANES, LANES), BF16),
    ]
    args = (places, meta, win)
    everyone = ep_count * obj_count
    for iteration in range(ITERS):
        coef_t, send = call(
            make_step_kernel(iteration == 0),
            (shaped((order, window_rows)), shaped((8 * group, LANES))),
            args,
            scratch=scratch,
            scalar=True,
            name=f"objects_{iteration}",
        )
        arrived = lax.all_to_all(
            send.reshape(group, 8, LANES), "obj", split_axis=0, concat_axis=0, tiled=True
        )
        lines = call(
            lambda a, o: mode_kernel(a, o, order=order),
            shaped((everyone, 1, LANES)),
            (arrived,),
            name=f"modes_{iteration}",
        )
        lines = lax.all_to_all(lines, ("ep", "obj"), split_axis=0, concat_axis=0, tiled=True)
        args = (places, meta, win, lines.reshape(everyone, LANES), coef_t)
    residual, power = call(
        lambda *refs: final_kernel(*refs, group=group),
        (shaped((rows, cols)), shaped((rows, width), BF16)),
        (*args, basis, light_curves),
        scratch=[
            pltpu.VMEM((ep_count, rows, LANES), F32),
            pltpu.VMEM((rows, span), BF16),
            pltpu.VMEM((rows, span), BF16),
        ],
        scalar=True,
        name="spectrum",
    )
    share = rows // ep_count
    power = lax.all_to_all(
        power.reshape(ep_count, share, width), "ep", split_axis=0, concat_axis=0, tiled=True
    )
    power = call(place_kernel, shaped((share, ep_count * width)), (power,), name="place")
    return residual, power


def solution(mesh):
    in_specs = (P("obj", "ep"), P("obj", "ep"), P("obj"), P("obj"), P("ep", None), P(), P())
    out_specs = (P("obj", "ep"), P(("obj", "ep"), None))
    return jax.shard_map(
        per_device, mesh=mesh, in_specs=in_specs, out_specs=out_specs, check_vma=False
    )
```

```python
import jax
import jax.numpy as jnp
import numpy as np
from jax import lax
from jax.experimental import pallas as pl
from jax.experimental.pallas import tpu as pltpu
from jax.sharding import PartitionSpec as P

ITERS = 2
HUBER = 1.345
DAMP = 2.0
RIDGE = 0.05
INVALID = 1e9
F32 = jnp.float32
BF16 = jnp.bfloat16
LANES = 128
VMEM = 14 << 20
CHUNKS = 4
NEAR = 1
EARLY = 1
SLAB = 256
PARTS = 4
NEAREST = 1.5 * 2.0**23
NT = (((1,), (1,)), ((), ()))
NN = (((1,), (0,)), ((), ()))


def dot(a, b, dims):
    return lax.dot_general(a, b, dims, preferred_element_type=F32)


def split2(x):
    hi = x.astype(BF16)
    lo = (x - hi.astype(F32)).astype(BF16)
    return hi, lo


def split3(x):
    hi = x.astype(BF16).astype(F32)
    rest = x - hi
    mid = rest.astype(BF16).astype(F32)
    low = (rest - mid).astype(BF16).astype(F32)
    return hi, mid, low


def solve_columns(rows, target):
    order = len(rows)
    half = order // 2
    rows = list(rows)
    scaled = [None] * order
    forward = [None] * order
    for k in range(order):
        at = k if k < half else k - half
        row = rows[k]
        inverse = 1.0 / (row[at : at + 1] + DAMP)
        unit = row * inverse
        scaled[k] = unit
        value = target[k : k + 1] * inverse
        forward[k] = value
        for i in range(k + 1, order):
            here = i if k < half else i - half
            factor = row[here : here + 1]
            if i >= half and k < half:
                rows[i] = rows[i] - factor * unit[half:]
            else:
                rows[i] = rows[i] - factor * unit
        if k < half:
            target = target - row * value
        else:
            target = jnp.concatenate([target[:half], target[half:] - row * value], axis=0)
    width = target.shape[1]
    level = lax.broadcasted_iota(jnp.int32, (half, width), 0)
    upper = jnp.zeros((half, width), F32)
    lower = jnp.zeros((half, width), F32)
    for k in reversed(range(order)):
        unit = scaled[k]
        if k >= half:
            value = forward[k] - jnp.sum(unit * lower, axis=0, keepdims=True)
            lower = jnp.where(level == k - half, value, lower)
        else:
            both = unit[:half] * upper + unit[half:] * lower
            value = forward[k] - jnp.sum(both, axis=0, keepdims=True)
            upper = jnp.where(level == k, value, upper)
    return jnp.concatenate([upper, lower], axis=0)


def outer_rows(x):
    half = x.shape[0] // 2
    upper = [x[i : i + 1] * x for i in range(half)]
    lower = [x[i : i + 1] * x[half:] for i in range(half, 2 * half)]
    return jnp.concatenate(upper + lower, axis=0)


def rows_of(gram, order):
    half = order // 2
    top = [gram[order * i : order * (i + 1)] for i in range(half)]
    start = order * half
    return top + [gram[start + half * i : start + half * (i + 1)] for i in range(half)]


def coef_factors(coef_t):
    order = coef_t.shape[0]
    hi, mid, low = split3(coef_t)
    none = jnp.zeros((LANES - 6 * order, coef_t.shape[1]), F32)
    stack = jnp.concatenate([hi, mid, low, hi, mid, hi, none], axis=0)
    return stack.T.astype(BF16)


def mode_factors(modes_b):
    order = modes_b.shape[0]
    hi, mid, low = split3(modes_b)
    none = jnp.zeros((LANES - 6 * order, modes_b.shape[1]), F32)
    return jnp.concatenate([hi, hi, hi, mid, mid, low, none], axis=0).astype(BF16)


def window(meta):
    rows = meta.shape[1]
    filled = jnp.concatenate([meta, jnp.zeros((LANES - meta.shape[0], rows), F32)], axis=0)
    turned = filled.T
    same = (turned[:, 0:1] == meta[0:1]).astype(F32).astype(BF16)
    return same, turned[:, 1:2]


def block_of(win_ref, b, own_rows, order):
    coded = jnp.concatenate([win_ref[b, :own_rows], win_ref[b, own_rows + order :]], axis=0)
    ok = coded < 0.5 * INVALID
    return ok, jnp.where(ok, coded, 0.0)


def pixel_total(same, part):
    hi, mid, low = split3(part)
    wide = jnp.concatenate([hi, mid, low], axis=1).astype(BF16)
    total = dot(same, wide, NN)
    total = total[:, :LANES] + total[:, LANES : 2 * LANES] + total[:, 2 * LANES :]
    return jnp.sum(total, axis=1, keepdims=True)


def spread_of(same, part, count):
    return jnp.sqrt(pixel_total(same, part) / jnp.maximum(count, 1.0) + 1e-06)


def robust_weight(ok, scaled, edge, sigma):
    return jnp.where(ok, (sigma * sigma) * (edge / jnp.maximum(jnp.abs(scaled), edge)), 0.0)


def natural_modes(arrived, blocks, group, order):
    turns = LANES // group
    lane = lax.broadcasted_iota(jnp.int32, (order, LANES), 1)
    turned = arrived.T
    out = []
    for b in range(blocks):
        tile, inner = divmod(b * group, LANES)
        total = jnp.zeros((order, LANES), F32)
        for r in range(turns):
            piece = turned[order * r : order * (r + 1), LANES * tile : LANES * (tile + 1)]
            shift = (group * r - inner) % LANES
            if shift:
                piece = pltpu.roll(piece, shift, 1)
            inside = (lane >= group * r) & (lane < group * (r + 1))
            total = jnp.where(inside, piece, total)
        out.append(total)
    return out


def prep_kernel(lc_hbm, valid_hbm, pix_hbm, sig_hbm, init_hbm, own_ref, tail_ref, head_ref,
                lc_ref, valid_ref, pix_ref, sig_ref, init_ref, sems):
    pairs = (
        (lc_hbm, lc_ref), (valid_hbm, valid_ref), (pix_hbm, pix_ref), (sig_hbm, sig_ref), (init_hbm, init_ref)
    )
    copies = [pltpu.make_async_copy(a, b, sems.at[i]) for i, (a, b) in enumerate(pairs)]
    for copy in copies:
        copy.start()
    for copy in copies:
        copy.wait()
    rows = lc_ref.shape[0]
    half = rows // 2
    coded = jnp.where(valid_ref[...] != 0, lc_ref[...], INVALID)
    own_ref[:rows] = coded
    own_ref[rows:] = init_ref[...]
    meta = jnp.concatenate(
        [pix_ref[...].astype(F32), sig_ref[...], jnp.zeros((6, rows), F32)], axis=0
    )
    tail_ref[:half] = coded[half:]
    tail_ref[half:] = meta
    head_ref[:half] = coded[:half]
    head_ref[half:] = meta


def widen_kernel(own_ref, tail_ref, left_ref, right_ref, out_ref, meta_ref):
    rows = tail_ref.shape[1]
    half = rows // 2
    own = own_ref[...]
    top = own.shape[0]
    left = left_ref[...]
    right = right_ref[...]
    for b in range(out_ref.shape[0]):
        out_ref[b, :top] = own
        out_ref[b, top : top + half] = left[:half]
        out_ref[b, top + half :] = right[:half]
    lane = lax.broadcasted_iota(jnp.int32, (8, rows), 1)
    beyond = pltpu.roll(jnp.where(lane >= half, left[half:], right[half:]), half, 1)
    meta_ref[:, :rows] = tail_ref[half:]
    meta_ref[:, rows:] = beyond


def make_step_kernel(first):
    def kernel(*refs):
        if first:
            place_ref, meta_ref, win_ref = refs[:3]
            rest = refs[3:]
        else:
            place_ref, meta_ref, win_ref, arrived_ref, before_ref = refs[:5]
            rest = refs[5:]
        coef_ref, send_ref, scal_ref, wh_ref, wl_ref, ph_ref, pl_ref, oh_ref, ol_ref, mh_ref, ml_ref, ms_ref = rest
        blocks = win_ref.shape[0]
        order = coef_ref.shape[0]
        rows = meta_ref.shape[1]
        own_rows = rows // 2
        group = send_ref.shape[0] // 8
        same, sigma = window(meta_ref[...])
        if first:
            modes = [win_ref[b, own_rows : own_rows + order] for b in range(blocks)]
        else:
            modes = natural_modes(arrived_ref[...], blocks, group, order)
            factors = coef_factors(before_ref[...])
        part = jnp.zeros((rows, LANES), F32)
        seen = jnp.zeros((rows, LANES), F32)
        for b in range(blocks):
            ok, lc = block_of(win_ref, b, own_rows, order)
            ms_ref[b] = mode_factors(modes[b])
            if not first:
                lc = lc - dot(factors, ms_ref[b], NN)
            scaled = lc * sigma
            scal_ref[b] = scaled
            part = part + jnp.where(ok, scaled * scaled, 0.0)
            seen = seen + jnp.where(ok, 1.0, 0.0)
        count = jnp.sum(dot(same, seen.astype(BF16), NN), axis=1, keepdims=True)
        edge = HUBER * spread_of(same, part, count)
        for b in range(blocks):
            ok, lc = block_of(win_ref, b, own_rows, order)
            weight = robust_weight(ok, scal_ref[b], edge, sigma)
            at = slice(LANES * b, LANES * (b + 1))
            wh_ref[:, at], wl_ref[:, at] = split2(weight)
            ph_ref[:, at], pl_ref[:, at] = split2(weight * lc)
            oh_ref[:, at], ol_ref[:, at] = split2(outer_rows(modes[b]))
            mh_ref[:, at], ml_ref[:, at] = split2(modes[b])
        gram = (
            dot(oh_ref[...], wh_ref[...], NT)
            + dot(oh_ref[...], wl_ref[...], NT)
            + dot(ol_ref[...], wh_ref[...], NT)
        )
        target = (
            dot(mh_ref[...], ph_ref[...], NT)
            + dot(mh_ref[...], pl_ref[...], NT)
            + dot(ml_ref[...], ph_ref[...], NT)
        )
        coef_t = solve_columns(rows_of(gram, order), target)
        coef_ref[...] = coef_t
        factors = coef_factors(coef_t)
        part = jnp.zeros((rows, LANES), F32)
        for b in range(blocks):
            ok, lc = block_of(win_ref, b, own_rows, order)
            scaled = (lc - dot(factors, ms_ref[b], NN)) * sigma
            scal_ref[b] = scaled
            part = part + jnp.where(ok, scaled * scaled, 0.0)
        edge = HUBER * spread_of(same, part, count)
        place = place_ref[0]
        coded = win_ref[place, :own_rows]
        ok = coded < 0.5 * INVALID
        lc = jnp.where(ok, coded, 0.0)
        weight = robust_weight(ok, scal_ref[place, :own_rows], edge[:own_rows], sigma[:own_rows])
        weight_hi, weight_lo = split2(weight)
        value_hi, value_lo = split2(weight * lc)
        own_coef = coef_t[:, :own_rows]
        outer_hi, outer_lo = split2(outer_rows(own_coef))
        coef_hi, coef_lo = split2(own_coef)
        gram = dot(outer_hi, weight_hi, NN) + dot(outer_hi, weight_lo, NN) + dot(outer_lo, weight_hi, NN)
        target = dot(coef_hi, value_hi, NN) + dot(coef_hi, value_lo, NN) + dot(coef_lo, value_hi, NN)
        spare = jnp.zeros((2 * LANES - gram.shape[0] - order, LANES), F32)
        tall = jnp.concatenate([gram, target, spare], axis=0)
        turns = LANES // group
        for side in range(2):
            turned = tall[LANES * side : LANES * (side + 1)].T
            for r in range(turns):
                send_ref[pl.ds(turns * side + r, group, stride=8), :] = turned[group * r : group * (r + 1)]

    return kernel


def mode_kernel(arrived_ref, out_ref, *, order):
    total = arrived_ref[0]
    for j in range(1, arrived_ref.shape[0]):
        total = total + arrived_ref[j]
    turns = total.shape[0] // 2
    tall = jnp.concatenate([total, jnp.zeros((LANES - 2 * turns, LANES), F32)], axis=0).T
    after = pltpu.roll(tall, LANES - turns, 1)
    half = order // 2
    gram = jnp.concatenate([tall, after[: half * half]], axis=0)
    target = after[half * half : half * half + order]
    solved = solve_columns(rows_of(gram, order), target)
    lane = lax.broadcasted_iota(jnp.int32, solved.shape, 1)
    solved = jnp.where(lane < turns, solved, 0.0)
    wide = jnp.concatenate([solved, jnp.zeros((LANES - order, LANES), F32)], axis=0).T
    line = wide[0:1]
    for r in range(1, turns):
        line = line + pltpu.roll(wide[0:8], order * r, 1)[r : r + 1]
    out_ref[...] = jnp.broadcast_to(line.reshape(1, 1, LANES), out_ref.shape)


def half_turn_series():
    grid = (np.cos(np.pi * (np.arange(400) + 0.5) / 400) + 1) / 2
    u = np.sqrt(grid) / 2
    sine = np.polynomial.polynomial.polyfit(grid, np.sin(np.pi * u) / u, 4)
    cosine = np.polynomial.polynomial.polyfit(grid, np.cos(np.pi * u), 5)
    return [float(c) * 4.0**k for k, c in enumerate(sine)], [float(c) * 4.0**k for k, c in enumerate(cosine)]


SINE, COSINE = half_turn_series()


def horner(series, x):
    total = x * series[-1] + series[-2]
    for c in series[-3::-1]:
        total = total * x + c
    return total


def basis_kernel(jitter_ref, freq_ref, *rest):
    (out_ref, time_ref), far = (rest, None) if len(rest) == 2 else ((rest[2], rest[1]), rest)
    blocks, width = jitter_ref.shape[0], freq_ref.shape[1]
    jitter = jnp.concatenate([jitter_ref[...], jnp.zeros((LANES - blocks, LANES), F32)], axis=0).T
    index = lax.broadcasted_iota(jnp.int32, (LANES, LANES), 0)
    for b in range(blocks):
        time_ref[LANES * b : LANES * (b + 1)] = (index + LANES * b).astype(F32) + jitter[:, b : b + 1]
    step = 32

    def copy(b):
        at = pl.ds(pl.multiple_of(LANES * b, LANES), LANES)
        return pltpu.make_async_copy(out_ref.at[at], far[0].at[at], far[3].at[b])

    def rows_from(i):
        at = pl.ds(pl.multiple_of(step * i, step), step)
        times = time_ref[at]
        for c in range(width // LANES):
            cycles = times * freq_ref[:, LANES * c : LANES * (c + 1)]
            turn = cycles - ((cycles + NEAREST) - NEAREST)
            square = turn * turn
            sine = turn * horner(SINE, square)
            cosine = horner(COSINE, square)
            twice = sine + sine
            start = LANES * c
            out_ref[at, start : start + LANES] = (1.0 - twice * sine).astype(BF16)
            out_ref[at, start + width : start + width + LANES] = (twice * cosine).astype(BF16)

    @pl.loop(0, blocks)
    def _(b):
        @pl.loop(0, LANES // step)
        def _(i):
            rows_from(b * (LANES // step) + i)

        if far:
            copy(b).start()

    if far:

        @pl.loop(0, blocks)
        def _(b):
            copy(b).wait()


def final_kernel(place_ref, meta_ref, win_ref, arrived_ref, coef_ref, lc_ref, *rest, group):
    far, (resid_ref, power_ref, res_ref, col_ref, both_ref) = rest[:CHUNKS], rest[CHUNKS : CHUNKS + 5]
    basis_refs, sems = far[:NEAR] + rest[CHUNKS + 5 : -1], rest[-1]
    copies = [None] * (PARTS * NEAR)
    for c in range(NEAR, CHUNKS):
        tall = basis_refs[c].shape[0] // PARTS
        for k in range(PARTS):
            at = pl.ds(tall * k, tall)
            copies.append(pltpu.make_async_copy(far[c].at[at], basis_refs[c].at[at], sems.at[c * PARTS + k]))
            copies[-1].start()
    blocks = win_ref.shape[0]
    order = coef_ref.shape[0]
    rows = meta_ref.shape[1]
    own_rows = rows // 2
    share = power_ref.shape[0]
    same, sigma = window(meta_ref[...])
    modes = natural_modes(arrived_ref[...], blocks, group, order)
    factors = coef_factors(coef_ref[...])
    part = jnp.zeros((rows, LANES), F32)
    seen = jnp.zeros((rows, LANES), F32)
    for b in range(blocks):
        ok, lc = block_of(win_ref, b, own_rows, order)
        resid = lc - dot(factors, mode_factors(modes[b]), NN)
        res_ref[b] = resid[:own_rows]
        scaled = resid * sigma
        part = part + jnp.where(ok, scaled * scaled, 0.0)
        seen = seen + jnp.where(ok, 1.0, 0.0)
    count = jnp.sum(dot(same, seen.astype(BF16), NN), axis=1, keepdims=True)
    edge = HUBER * spread_of(same, part, count)
    col_ref[0] = jnp.broadcast_to(edge[:own_rows], (own_rows, LANES))
    col_ref[1] = jnp.broadcast_to(sigma[:own_rows], (own_rows, LANES))
    place = place_ref[0]
    ok = win_ref[place, :own_rows] < 0.5 * INVALID
    resid = res_ref[place]
    resid_ref[...] = jnp.where(ok, resid, lc_ref[...] + resid)
    mine = pl.ds(pl.multiple_of(place * share, share), share)
    edge = col_ref[0, mine]
    sigma = col_ref[1, mine]
    total = jnp.zeros((share, LANES), F32)
    level = jnp.zeros((share, LANES), F32)
    for b in range(blocks):
        ok = win_ref[b, mine] < 0.5 * INVALID
        resid = res_ref[b, mine]
        weight = robust_weight(ok, resid * sigma, edge, sigma)
        at = slice(LANES * b, LANES * (b + 1))
        weight_b = weight.astype(BF16)
        value_b = (weight * resid).astype(BF16)
        both_ref[:share, at] = weight_b
        both_ref[share:, at] = value_b
        total = total + weight_b.astype(F32)
        level = level + value_b.astype(F32)
    total = jnp.sum(total, axis=1, keepdims=True)
    level = jnp.sum(level, axis=1, keepdims=True)
    inverse = 1.0 / total
    mean_level = level * inverse
    for c, basis_ref in enumerate(basis_refs):
        width = basis_ref.shape[1] // 2
        for copy in copies[PARTS * c : PARTS * (c + 1)] if c >= NEAR else ():
            copy.wait()
        single = jnp.zeros((2 * share, 2 * width), F32)
        double_cos = [jnp.zeros((share, SLAB), F32) for _ in range(width // SLAB)]
        double_sin = [jnp.zeros((share, SLAB), F32) for _ in range(width // SLAB)]
        for k in range(basis_ref.shape[0] // SLAB):
            at = slice(SLAB * k, SLAB * (k + 1))
            single = single + dot(both_ref[:, at], basis_ref[at], NN)
            for n in range(width // SLAB):
                cos_b = basis_ref[at, SLAB * n : SLAB * (n + 1)].astype(F32)
                sin_b = basis_ref[at, width + SLAB * n : width + SLAB * (n + 1)].astype(F32)
                twice = sin_b + sin_b
                cos_two = (1.0 - twice * sin_b).astype(BF16)
                sin_two = (twice * cos_b).astype(BF16)
                double_cos[n] = double_cos[n] + dot(both_ref[:share, at], cos_two, NN)
                double_sin[n] = double_sin[n] + dot(both_ref[:share, at], sin_two, NN)
        cosine = single[:share, :width]
        sine = single[:share, width:]
        cosine_two = jnp.concatenate(double_cos, axis=1)
        sine_two = jnp.concatenate(double_sin, axis=1)
        ycos = single[share:, :width] - mean_level * cosine
        ysin = single[share:, width:] - mean_level * sine
        cc_term = 0.5 * (total + cosine_two) - cosine * cosine * inverse + RIDGE * total
        ss_term = 0.5 * (total - cosine_two) - sine * sine * inverse + RIDGE * total
        cs_term = 0.5 * sine_two - cosine * sine * inverse
        determinant = cc_term * ss_term - cs_term * cs_term
        power = (ss_term * ycos * ycos + cc_term * ysin * ysin - 2.0 * cs_term * ycos * ysin) / determinant
        power_ref[:, width * c : width * (c + 1)] = power


def shaped(shape, dtype=F32):
    return jax.ShapeDtypeStruct(shape, dtype)


def call(kernel, out_shape, args, scratch=(), scalar=False, away=(), out_space=pltpu.VMEM, limit=VMEM, name=None):
    specs = [pl.BlockSpec(memory_space=pltpu.HBM if at in away else pltpu.VMEM) for at in range(len(args))]
    if scalar:
        specs[0] = pl.BlockSpec(memory_space=pltpu.SMEM)
    many = isinstance(out_shape, (tuple, list))
    out_specs = [pl.BlockSpec(memory_space=out_space) for _ in (out_shape if many else [0])]
    return pl.pallas_call(
        kernel,
        out_shape=out_shape,
        in_specs=specs,
        out_specs=out_specs if many else out_specs[0],
        scratch_shapes=list(scratch),
        compiler_params=pltpu.CompilerParams(vmem_limit_bytes=limit),
        name=name,
    )(*args)


def per_device(light_curves, valid, pixel, inv_sigma, modes_init, epoch_jitter, freq_index):
    obj_count = lax.axis_size("obj")
    ep_count = lax.axis_size("ep")
    rows, cols = light_curves.shape
    order = modes_init.shape[1]
    half = rows // 2
    span = ep_count * cols
    group = obj_count
    place = lax.axis_index("ep").astype(jnp.int32)
    places = place.reshape(1)

    fetched = (light_curves, valid, pixel.reshape(1, rows), inv_sigma.reshape(1, rows), modes_init.T)
    fetched = tuple(pltpu.with_memory_space_constraint(a, pltpu.HBM) for a in fetched)
    own, tail, head = call(
        prep_kernel,
        (shaped((rows + order, cols)), shaped((half + 8, cols)), shaped((half + 8, cols))),
        fetched,
        scratch=[pltpu.VMEM(a.shape, a.dtype) for a in fetched] + [pltpu.SemaphoreType.DMA((5,))],
        away=range(5),
        name="prep",
    )
    jitter = epoch_jitter.reshape(ep_count, cols)
    freqs = (freq_index + 1).astype(F32) / (4.0 * span)
    width = freqs.shape[0] // CHUNKS
    own, *pieces = lax.optimization_barrier(
        (own, *[freqs[width * c : width * (c + 1)].reshape(1, width) for c in range(CHUNKS)])
    )

    def basis_of(piece, far):
        scratch = [pltpu.VMEM((span, LANES), F32)]
        if far:
            scratch += [pltpu.VMEM((span, 2 * width), BF16), pltpu.SemaphoreType.DMA((ep_count,))]
        out = pltpu.HBM((span, 2 * width), BF16) if far else shaped((span, 2 * width), BF16)
        space = pltpu.HBM if far else pltpu.VMEM
        return call(basis_kernel, out, (jitter, piece), scratch=scratch, out_space=space, name="basis")

    ring = [(i, (i + 1) % obj_count) for i in range(obj_count)]
    back = [(i, (i - 1) % obj_count) for i in range(obj_count)]
    left = lax.ppermute(tail, "obj", ring)
    right = lax.ppermute(head, "obj", back)
    made = [basis_of(pieces.pop(0), c >= NEAR) for c in range(EARLY)]
    left, right, *made = lax.optimization_barrier((left, right, *made))
    wide, meta = call(
        widen_kernel,
        (shaped((ep_count, 2 * rows + order, cols)), shaped((8, 2 * rows))),
        (own, tail, left, right),
        name="widen",
    )
    wide, *pieces = lax.optimization_barrier((wide, *pieces))
    win = lax.all_to_all(wide, "ep", split_axis=0, concat_axis=0, tiled=True)
    win, *basis = lax.optimization_barrier((win, *(made + [basis_of(p, True) for p in pieces])))

    window_rows = 2 * rows
    products = order * order * 3 // 4
    scratch = [
        pltpu.VMEM((ep_count, window_rows, LANES), F32),
        pltpu.VMEM((window_rows, span), BF16),
        pltpu.VMEM((window_rows, span), BF16),
        pltpu.VMEM((window_rows, span), BF16),
        pltpu.VMEM((window_rows, span), BF16),
        pltpu.VMEM((products, span), BF16),
        pltpu.VMEM((products, span), BF16),
        pltpu.VMEM((order, span), BF16),
        pltpu.VMEM((order, span), BF16),
        pltpu.VMEM((ep_count, LANES, LANES), BF16),
    ]
    args = (places, meta, win)
    everyone = ep_count * obj_count
    for iteration in range(ITERS):
        coef_t, send = call(
            make_step_kernel(iteration == 0),
            (shaped((order, window_rows)), shaped((8 * group, LANES))),
            args,
            scratch=scratch,
            scalar=True,
            name=f"objects_{iteration}",
        )
        arrived = lax.all_to_all(
            send.reshape(group, 8, LANES), "obj", split_axis=0, concat_axis=0, tiled=True
        )
        lines = call(
            lambda a, o: mode_kernel(a, o, order=order),
            shaped((everyone, 1, LANES)),
            (arrived,),
            name=f"modes_{iteration}",
        )
        lines = lax.all_to_all(lines, ("ep", "obj"), split_axis=0, concat_axis=0, tiled=True)
        args = (places, meta, win, lines.reshape(everyone, LANES), coef_t)
    basis[NEAR:] = [pltpu.with_memory_space_constraint(b, pltpu.HBM) for b in basis[NEAR:]]
    residual, power = call(
        lambda *refs: final_kernel(*refs, group=group),
        (shaped((rows, cols)), shaped((rows // ep_count, freqs.shape[0]))),
        (*args, light_curves, *basis),
        scratch=[
            pltpu.VMEM((ep_count, rows, LANES), F32),
            pltpu.VMEM((2, rows, LANES), F32),
            pltpu.VMEM((2 * rows // ep_count, span), BF16),
            *[pltpu.VMEM((span, 2 * width), BF16) for _ in range(NEAR, CHUNKS)],
            pltpu.SemaphoreType.DMA((CHUNKS * PARTS,)),
        ],
        scalar=True,
        away=range(len(args) + 1 + NEAR, len(args) + 1 + CHUNKS),
        limit=32 << 20,
        name="spectrum",
    )
    return residual, power


def solution(mesh):
    in_specs = (P("obj", "ep"), P("obj", "ep"), P("obj"), P("obj"), P("ep", None), P(), P())
    out_specs = (P("obj", "ep"), P(("obj", "ep"), None))
    return jax.shard_map(
        per_device, mesh=mesh, in_specs=in_specs, out_specs=out_specs, check_vma=False
    )
```

```python
import jax
import jax.numpy as jnp
import numpy as np
from jax import lax
from jax.experimental import pallas as pl
from jax.experimental.pallas import tpu as pltpu
from jax.sharding import PartitionSpec as P

ITERS = 2
HUBER = 1.345
DAMP = 2.0
RIDGE = 0.05
INVALID = 1e9
F32 = jnp.float32
BF16 = jnp.bfloat16
LANES = 128
VMEM = 14 << 20
CHUNKS = 4
NEAR = 1
SLAB = 256
PARTS = 4
NEAREST = 1.5 * 2.0**23
NT = (((1,), (1,)), ((), ()))
NN = (((1,), (0,)), ((), ()))


def dot(a, b, dims):
    return lax.dot_general(a, b, dims, preferred_element_type=F32)


def split2(x):
    hi = x.astype(BF16)
    lo = (x - hi.astype(F32)).astype(BF16)
    return hi, lo


def split3(x):
    hi = x.astype(BF16).astype(F32)
    rest = x - hi
    mid = rest.astype(BF16).astype(F32)
    low = (rest - mid).astype(BF16).astype(F32)
    return hi, mid, low


def solve_columns(rows, target):
    order = len(rows)
    half = order // 2
    rows = list(rows)
    scaled = [None] * order
    forward = [None] * order
    for k in range(order):
        at = k if k < half else k - half
        row = rows[k]
        inverse = 1.0 / (row[at : at + 1] + DAMP)
        unit = row * inverse
        scaled[k] = unit
        value = target[k : k + 1] * inverse
        forward[k] = value
        for i in range(k + 1, order):
            here = i if k < half else i - half
            factor = row[here : here + 1]
            if i >= half and k < half:
                rows[i] = rows[i] - factor * unit[half:]
            else:
                rows[i] = rows[i] - factor * unit
        if k < half:
            target = target - row * value
        else:
            target = jnp.concatenate([target[:half], target[half:] - row * value], axis=0)
    width = target.shape[1]
    level = lax.broadcasted_iota(jnp.int32, (half, width), 0)
    upper = jnp.zeros((half, width), F32)
    lower = jnp.zeros((half, width), F32)
    for k in reversed(range(order)):
        unit = scaled[k]
        if k >= half:
            value = forward[k] - jnp.sum(unit * lower, axis=0, keepdims=True)
            lower = jnp.where(level == k - half, value, lower)
        else:
            both = unit[:half] * upper + unit[half:] * lower
            value = forward[k] - jnp.sum(both, axis=0, keepdims=True)
            upper = jnp.where(level == k, value, upper)
    return jnp.concatenate([upper, lower], axis=0)


def outer_rows(x):
    half = x.shape[0] // 2
    upper = [x[i : i + 1] * x for i in range(half)]
    lower = [x[i : i + 1] * x[half:] for i in range(half, 2 * half)]
    return jnp.concatenate(upper + lower, axis=0)


def rows_of(gram, order):
    half = order // 2
    top = [gram[order * i : order * (i + 1)] for i in range(half)]
    start = order * half
    return top + [gram[start + half * i : start + half * (i + 1)] for i in range(half)]


def coef_factors(coef_t):
    order = coef_t.shape[0]
    hi, mid, low = split3(coef_t)
    none = jnp.zeros((LANES - 6 * order, coef_t.shape[1]), F32)
    stack = jnp.concatenate([hi, mid, low, hi, mid, hi, none], axis=0)
    return stack.T.astype(BF16)


def mode_factors(modes_b):
    order = modes_b.shape[0]
    hi, mid, low = split3(modes_b)
    none = jnp.zeros((LANES - 6 * order, modes_b.shape[1]), F32)
    return jnp.concatenate([hi, hi, hi, mid, mid, low, none], axis=0).astype(BF16)


def window(meta):
    rows = meta.shape[1]
    filled = jnp.concatenate([meta, jnp.zeros((LANES - meta.shape[0], rows), F32)], axis=0)
    turned = filled.T
    same = (turned[:, 0:1] == meta[0:1]).astype(F32).astype(BF16)
    return same, turned[:, 1:2]


def own_of(win_ref, b, rows):
    coded = win_ref[b, :rows].astype(F32) + win_ref[b, rows : 2 * rows].astype(F32)
    ok = coded < 0.5 * INVALID
    return ok, jnp.where(ok, coded, 0.0)


def block_of(win_ref, b, rows):
    own = win_ref[b, :rows].astype(F32) + win_ref[b, rows : 2 * rows].astype(F32)
    coded = jnp.concatenate([own, win_ref[b, 2 * rows : 3 * rows].astype(F32)], axis=0)
    ok = coded < 0.5 * INVALID
    return ok, jnp.where(ok, coded, 0.0)


def first_modes(win_ref, b, rows, order):
    parts = win_ref[b, 3 * rows :].astype(F32)
    return parts[:order] + (parts[order : 2 * order] + parts[2 * order :])


def pixel_total(same, part):
    hi, mid, low = split3(part)
    wide = jnp.concatenate([hi, mid, low], axis=1).astype(BF16)
    total = dot(same, wide, NN)
    total = total[:, :LANES] + total[:, LANES : 2 * LANES] + total[:, 2 * LANES :]
    return jnp.sum(total, axis=1, keepdims=True)


def spread_of(same, part, count):
    return jnp.sqrt(pixel_total(same, part) / jnp.maximum(count, 1.0) + 1e-06)


def robust_weight(ok, scaled, edge, sigma):
    return jnp.where(ok, (sigma * sigma) * (edge / jnp.maximum(jnp.abs(scaled), edge)), 0.0)


def natural_modes(arrived, blocks, group, order):
    turns = LANES // group
    lane = lax.broadcasted_iota(jnp.int32, (order, LANES), 1)
    turned = arrived.T
    out = []
    for b in range(blocks):
        tile, inner = divmod(b * group, LANES)
        total = jnp.zeros((order, LANES), F32)
        for r in range(turns):
            piece = turned[order * r : order * (r + 1), LANES * tile : LANES * (tile + 1)]
            shift = (group * r - inner) % LANES
            if shift:
                piece = pltpu.roll(piece, shift, 1)
            inside = (lane >= group * r) & (lane < group * (r + 1))
            total = jnp.where(inside, piece, total)
        out.append(total)
    return out


def prep_kernel(lc_hbm, valid_hbm, pix_hbm, sig_hbm, init_hbm, own_ref, tail_ref, head_ref,
                lc_ref, valid_ref, pix_ref, sig_ref, init_ref, sems):
    pairs = (
        (lc_hbm, lc_ref), (valid_hbm, valid_ref), (pix_hbm, pix_ref), (sig_hbm, sig_ref), (init_hbm, init_ref)
    )
    copies = [pltpu.make_async_copy(a, b, sems.at[i]) for i, (a, b) in enumerate(pairs)]
    for copy in copies:
        copy.start()
    for copy in copies:
        copy.wait()
    rows = lc_ref.shape[0]
    half = rows // 2
    coded = jnp.where(valid_ref[...] != 0, lc_ref[...], INVALID)
    own_ref[:rows], own_ref[rows : 2 * rows] = split2(coded)
    own_ref[2 * rows :] = jnp.concatenate(split3(init_ref[...]), axis=0).astype(BF16)
    meta = jnp.concatenate(
        [pix_ref[...].astype(F32), sig_ref[...], jnp.zeros((6, rows), F32)], axis=0
    )
    tail_ref[:half] = coded[half:]
    tail_ref[half:] = meta
    head_ref[:half] = coded[:half]
    head_ref[half:] = meta


def widen_kernel(own_ref, tail_ref, left_ref, right_ref, out_hbm, meta_ref, one_ref, sems):
    rows = tail_ref.shape[1]
    half = rows // 2
    left = left_ref[...]
    right = right_ref[...]
    one_ref[: 2 * rows] = own_ref[: 2 * rows]
    one_ref[2 * rows : 3 * rows] = jnp.concatenate([left[:half], right[:half]], axis=0).astype(BF16)
    one_ref[3 * rows :] = own_ref[2 * rows :]
    copies = [pltpu.make_async_copy(one_ref, out_hbm.at[b], sems.at[b]) for b in range(out_hbm.shape[0])]
    for copy in copies:
        copy.start()
    lane = lax.broadcasted_iota(jnp.int32, (8, rows), 1)
    beyond = pltpu.roll(jnp.where(lane >= half, left[half:], right[half:]), half, 1)
    meta_ref[:, :rows] = tail_ref[half:]
    meta_ref[:, rows:] = beyond
    for copy in copies:
        copy.wait()


def make_step_kernel(first):
    def kernel(*refs):
        if first:
            place_ref, meta_ref, win_ref = refs[:3]
            rest = refs[3:]
        else:
            place_ref, meta_ref, win_ref, arrived_ref, before_ref = refs[:5]
            rest = refs[5:]
        coef_ref, send_ref, scal_ref, wh_ref, wl_ref, ph_ref, pl_ref, oh_ref, ol_ref, mh_ref, ml_ref, ms_ref = rest
        blocks = win_ref.shape[0]
        order = coef_ref.shape[0]
        rows = meta_ref.shape[1]
        own_rows = rows // 2
        group = send_ref.shape[0] // 8
        same, sigma = window(meta_ref[...])
        if first:
            modes = [first_modes(win_ref, b, own_rows, order) for b in range(blocks)]
        else:
            modes = natural_modes(arrived_ref[...], blocks, group, order)
            factors = coef_factors(before_ref[...])
        part = jnp.zeros((rows, LANES), F32)
        seen = jnp.zeros((rows, LANES), F32)
        for b in range(blocks):
            ok, lc = block_of(win_ref, b, own_rows)
            ms_ref[b] = mode_factors(modes[b])
            if not first:
                lc = lc - dot(factors, ms_ref[b], NN)
            scaled = lc * sigma
            scal_ref[b] = scaled
            part = part + jnp.where(ok, scaled * scaled, 0.0)
            seen = seen + jnp.where(ok, 1.0, 0.0)
        count = jnp.sum(dot(same, seen.astype(BF16), NN), axis=1, keepdims=True)
        edge = HUBER * spread_of(same, part, count)
        for b in range(blocks):
            ok, lc = block_of(win_ref, b, own_rows)
            weight = robust_weight(ok, scal_ref[b], edge, sigma)
            at = slice(LANES * b, LANES * (b + 1))
            wh_ref[:, at], wl_ref[:, at] = split2(weight)
            ph_ref[:, at], pl_ref[:, at] = split2(weight * lc)
            oh_ref[:, at], ol_ref[:, at] = split2(outer_rows(modes[b]))
            mh_ref[:, at], ml_ref[:, at] = split2(modes[b])
        gram = (
            dot(oh_ref[...], wh_ref[...], NT)
            + dot(oh_ref[...], wl_ref[...], NT)
            + dot(ol_ref[...], wh_ref[...], NT)
        )
        target = (
            dot(mh_ref[...], ph_ref[...], NT)
            + dot(mh_ref[...], pl_ref[...], NT)
            + dot(ml_ref[...], ph_ref[...], NT)
        )
        coef_t = solve_columns(rows_of(gram, order), target)
        coef_ref[...] = coef_t
        factors = coef_factors(coef_t)
        part = jnp.zeros((rows, LANES), F32)
        for b in range(blocks):
            ok, lc = block_of(win_ref, b, own_rows)
            scaled = (lc - dot(factors, ms_ref[b], NN)) * sigma
            scal_ref[b] = scaled
            part = part + jnp.where(ok, scaled * scaled, 0.0)
        edge = HUBER * spread_of(same, part, count)
        place = place_ref[0]
        ok, lc = own_of(win_ref, place, own_rows)
        weight = robust_weight(ok, scal_ref[place, :own_rows], edge[:own_rows], sigma[:own_rows])
        weight_hi, weight_lo = split2(weight)
        value_hi, value_lo = split2(weight * lc)
        own_coef = coef_t[:, :own_rows]
        outer_hi, outer_lo = split2(outer_rows(own_coef))
        coef_hi, coef_lo = split2(own_coef)
        gram = dot(outer_hi, weight_hi, NN) + dot(outer_hi, weight_lo, NN) + dot(outer_lo, weight_hi, NN)
        target = dot(coef_hi, value_hi, NN) + dot(coef_hi, value_lo, NN) + dot(coef_lo, value_hi, NN)
        spare = jnp.zeros((2 * LANES - gram.shape[0] - order, LANES), F32)
        tall = jnp.concatenate([gram, target, spare], axis=0)
        turns = LANES // group
        for side in range(2):
            turned = tall[LANES * side : LANES * (side + 1)].T
            for r in range(turns):
                send_ref[pl.ds(turns * side + r, group, stride=8), :] = turned[group * r : group * (r + 1)]

    return kernel


def mode_kernel(arrived_ref, out_ref, *, order):
    total = arrived_ref[0]
    for j in range(1, arrived_ref.shape[0]):
        total = total + arrived_ref[j]
    turns = total.shape[0] // 2
    tall = jnp.concatenate([total, jnp.zeros((LANES - 2 * turns, LANES), F32)], axis=0).T
    after = pltpu.roll(tall, LANES - turns, 1)
    half = order // 2
    gram = jnp.concatenate([tall, after[: half * half]], axis=0)
    target = after[half * half : half * half + order]
    solved = solve_columns(rows_of(gram, order), target)
    lane = lax.broadcasted_iota(jnp.int32, solved.shape, 1)
    solved = jnp.where(lane < turns, solved, 0.0)
    wide = jnp.concatenate([solved, jnp.zeros((LANES - order, LANES), F32)], axis=0).T
    line = wide[0:1]
    for r in range(1, turns):
        line = line + pltpu.roll(wide[0:8], order * r, 1)[r : r + 1]
    out_ref[...] = jnp.broadcast_to(line.reshape(1, 1, LANES), out_ref.shape)


def half_turn_series():
    grid = (np.cos(np.pi * (np.arange(400) + 0.5) / 400) + 1) / 2
    u = np.sqrt(grid) / 2
    sine = np.polynomial.polynomial.polyfit(grid, np.sin(np.pi * u) / u, 4)
    cosine = np.polynomial.polynomial.polyfit(grid, np.cos(np.pi * u), 5)
    return [float(c) * 4.0**k for k, c in enumerate(sine)], [float(c) * 4.0**k for k, c in enumerate(cosine)]


SINE, COSINE = half_turn_series()


def horner(series, x):
    total = x * series[-1] + series[-2]
    for c in series[-3::-1]:
        total = total * x + c
    return total


def basis_kernel(jitter_ref, index_ref, *rest, pieces, far):
    count = len(pieces)
    time_ref = rest[count]
    made = rest[count + 1 : 2 * count + 1] if far else rest[:count]
    blocks, width = jitter_ref.shape[0], index_ref.shape[1]
    freqs = (index_ref[...] + 1).astype(F32) / (4.0 * time_ref.shape[0])
    jitter = jnp.concatenate([jitter_ref[...], jnp.zeros((LANES - blocks, LANES), F32)], axis=0).T
    index = lax.broadcasted_iota(jnp.int32, (LANES, LANES), 0)
    for b in range(blocks):
        time_ref[LANES * b : LANES * (b + 1)] = (index + LANES * b).astype(F32) + jitter[:, b : b + 1]
    step = 32

    def copy(c, b):
        at = pl.ds(pl.multiple_of(LANES * b, LANES), LANES)
        return pltpu.make_async_copy(made[c].at[at], rest[c].at[at], rest[-1].at[c, b])

    @pl.loop(0, blocks)
    def _(b):
        @pl.loop(0, LANES // step)
        def _(i):
            at = pl.ds(pl.multiple_of(LANES * b + step * i, step), step)
            times = time_ref[at]
            for c in range(count):
                for n in range(width // LANES):
                    cycles = times * freqs[pieces[c] : pieces[c] + 1, LANES * n : LANES * (n + 1)]
                    turn = cycles - ((cycles + NEAREST) - NEAREST)
                    square = turn * turn
                    sine = turn * horner(SINE, square)
                    cosine = horner(COSINE, square)
                    twice = sine + sine
                    start = LANES * n
                    made[c][at, start : start + LANES] = (1.0 - twice * sine).astype(BF16)
                    made[c][at, start + width : start + width + LANES] = (twice * cosine).astype(BF16)

        if far:
            for c in range(count):
                copy(c, b).start()

    if far:

        @pl.loop(0, blocks)
        def _(b):
            for c in range(count):
                copy(c, b).wait()


def final_kernel(place_ref, meta_ref, win_ref, arrived_ref, coef_ref, lc_ref, *rest, group):
    far, (resid_ref, power_ref, res_ref, col_ref, both_ref) = rest[:CHUNKS], rest[CHUNKS : CHUNKS + 5]
    basis_refs, sems = far[:NEAR] + rest[CHUNKS + 5 : -1], rest[-1]
    copies = [None] * (PARTS * NEAR)
    for c in range(NEAR, CHUNKS):
        tall = basis_refs[c].shape[0] // PARTS
        for k in range(PARTS):
            at = pl.ds(tall * k, tall)
            copies.append(pltpu.make_async_copy(far[c].at[at], basis_refs[c].at[at], sems.at[c * PARTS + k]))
            copies[-1].start()
    blocks = win_ref.shape[0]
    order = coef_ref.shape[0]
    rows = meta_ref.shape[1]
    own_rows = rows // 2
    share = power_ref.shape[0]
    same, sigma = window(meta_ref[...])
    modes = natural_modes(arrived_ref[...], blocks, group, order)
    factors = coef_factors(coef_ref[...])
    part = jnp.zeros((rows, LANES), F32)
    seen = jnp.zeros((rows, LANES), F32)
    for b in range(blocks):
        ok, lc = block_of(win_ref, b, own_rows)
        resid = lc - dot(factors, mode_factors(modes[b]), NN)
        res_ref[b] = resid[:own_rows]
        scaled = resid * sigma
        part = part + jnp.where(ok, scaled * scaled, 0.0)
        seen = seen + jnp.where(ok, 1.0, 0.0)
    count = jnp.sum(dot(same, seen.astype(BF16), NN), axis=1, keepdims=True)
    edge = HUBER * spread_of(same, part, count)
    col_ref[0] = jnp.broadcast_to(edge[:own_rows], (own_rows, LANES))
    col_ref[1] = jnp.broadcast_to(sigma[:own_rows], (own_rows, LANES))
    place = place_ref[0]
    ok, lc = own_of(win_ref, place, own_rows)
    resid_ref[...] = lc_ref[...] - (lc - res_ref[place])
    mine = pl.ds(pl.multiple_of(place * share, share), share)
    edge = col_ref[0, mine]
    sigma = col_ref[1, mine]
    total = jnp.zeros((share, LANES), F32)
    level = jnp.zeros((share, LANES), F32)
    for b in range(blocks):
        ok = win_ref[b, mine].astype(F32) < 0.5 * INVALID
        resid = res_ref[b, mine]
        weight = robust_weight(ok, resid * sigma, edge, sigma)
        at = slice(LANES * b, LANES * (b + 1))
        weight_b = weight.astype(BF16)
        value_b = (weight * resid).astype(BF16)
        both_ref[:share, at] = weight_b
        both_ref[share:, at] = value_b
        total = total + weight_b.astype(F32)
        level = level + value_b.astype(F32)
    total = jnp.sum(total, axis=1, keepdims=True)
    level = jnp.sum(level, axis=1, keepdims=True)
    inverse = 1.0 / total
    mean_level = level * inverse
    for c, basis_ref in enumerate(basis_refs):
        width = basis_ref.shape[1] // 2
        for copy in copies[PARTS * c : PARTS * (c + 1)] if c >= NEAR else ():
            copy.wait()
        single = jnp.zeros((2 * share, 2 * width), F32)
        double_cos = [jnp.zeros((share, SLAB), F32) for _ in range(width // SLAB)]
        double_sin = [jnp.zeros((share, SLAB), F32) for _ in range(width // SLAB)]
        for k in range(basis_ref.shape[0] // SLAB):
            at = slice(SLAB * k, SLAB * (k + 1))
            single = single + dot(both_ref[:, at], basis_ref[at], NN)
            for n in range(width // SLAB):
                cos_b = basis_ref[at, SLAB * n : SLAB * (n + 1)].astype(F32)
                sin_b = basis_ref[at, width + SLAB * n : width + SLAB * (n + 1)].astype(F32)
                twice = sin_b + sin_b
                cos_two = (1.0 - twice * sin_b).astype(BF16)
                sin_two = (twice * cos_b).astype(BF16)
                double_cos[n] = double_cos[n] + dot(both_ref[:share, at], cos_two, NN)
                double_sin[n] = double_sin[n] + dot(both_ref[:share, at], sin_two, NN)
        cosine = single[:share, :width]
        sine = single[:share, width:]
        cosine_two = jnp.concatenate(double_cos, axis=1)
        sine_two = jnp.concatenate(double_sin, axis=1)
        ycos = single[share:, :width] - mean_level * cosine
        ysin = single[share:, width:] - mean_level * sine
        cc_term = 0.5 * (total + cosine_two) - cosine * cosine * inverse + RIDGE * total
        ss_term = 0.5 * (total - cosine_two) - sine * sine * inverse + RIDGE * total
        cs_term = 0.5 * sine_two - cosine * sine * inverse
        determinant = cc_term * ss_term - cs_term * cs_term
        power = (ss_term * ycos * ycos + cc_term * ysin * ysin - 2.0 * cs_term * ycos * ysin) / determinant
        power_ref[:, width * c : width * (c + 1)] = power


def shaped(shape, dtype=F32):
    return jax.ShapeDtypeStruct(shape, dtype)


def call(kernel, out_shape, args, scratch=(), scalar=False, away=(), out_space=pltpu.VMEM, limit=VMEM, name=None):
    specs = [pl.BlockSpec(memory_space=pltpu.HBM if at in away else pltpu.VMEM) for at in range(len(args))]
    if scalar:
        specs[0] = pl.BlockSpec(memory_space=pltpu.SMEM)
    many = isinstance(out_shape, (tuple, list))
    spaces = out_space if isinstance(out_space, (tuple, list)) else [out_space] * (len(out_shape) if many else 1)
    out_specs = [pl.BlockSpec(memory_space=space) for space in spaces]
    return pl.pallas_call(
        kernel,
        out_shape=out_shape,
        in_specs=specs,
        out_specs=out_specs if many else out_specs[0],
        scratch_shapes=list(scratch),
        compiler_params=pltpu.CompilerParams(vmem_limit_bytes=limit),
        name=name,
    )(*args)


def per_device(light_curves, valid, pixel, inv_sigma, modes_init, epoch_jitter, freq_index):
    obj_count = lax.axis_size("obj")
    ep_count = lax.axis_size("ep")
    rows, cols = light_curves.shape
    order = modes_init.shape[1]
    half = rows // 2
    span = ep_count * cols
    group = obj_count
    place = lax.axis_index("ep").astype(jnp.int32)
    places = place.reshape(1)

    fetched = (light_curves, valid, pixel.reshape(1, rows), inv_sigma.reshape(1, rows), modes_init.T)
    fetched = tuple(pltpu.with_memory_space_constraint(a, pltpu.HBM) for a in fetched)
    own, tail, head = call(
        prep_kernel,
        (shaped((2 * rows + 3 * order, cols), BF16), shaped((half + 8, cols)), shaped((half + 8, cols))),
        fetched,
        scratch=[pltpu.VMEM(a.shape, a.dtype) for a in fetched] + [pltpu.SemaphoreType.DMA((5,))],
        away=range(5),
        name="prep",
    )
    ring = [(i, (i + 1) % obj_count) for i in range(obj_count)]
    back = [(i, (i - 1) % obj_count) for i in range(obj_count)]
    left = lax.ppermute(tail, "obj", ring)
    right = lax.ppermute(head, "obj", back)
    shape = (ep_count, 3 * (rows + order), cols)
    wide, meta = call(
        widen_kernel,
        (pltpu.HBM(shape, BF16), shaped((8, 2 * rows))),
        (own, tail, left, right),
        scratch=[pltpu.VMEM(shape[1:], BF16), pltpu.SemaphoreType.DMA((ep_count,))],
        out_space=(pltpu.HBM, pltpu.VMEM),
        name="widen",
    )

    width = freq_index.shape[0] // CHUNKS
    jitter = epoch_jitter.reshape(ep_count, cols)

    index = freq_index.reshape(CHUNKS, width)

    def basis_of(index, pieces, far):
        scratch = [pltpu.VMEM((span, LANES), F32)]
        if far:
            scratch += [pltpu.VMEM((span, 2 * width), BF16) for _ in pieces]
            scratch += [pltpu.SemaphoreType.DMA((len(pieces), ep_count))]
        place_of = pltpu.HBM if far else shaped
        return call(
            lambda *refs: basis_kernel(*refs, pieces=pieces, far=far),
            [place_of((span, 2 * width), BF16) for _ in pieces],
            (jitter, index),
            scratch=scratch,
            out_space=[pltpu.HBM if far else pltpu.VMEM] * len(pieces),
            name="basis",
        )

    wide, index = lax.optimization_barrier((wide, index))
    win = lax.all_to_all(wide, "ep", split_axis=0, concat_axis=0, tiled=True)
    win, *basis = lax.optimization_barrier((win, *basis_of(index, range(NEAR, CHUNKS), True)))

    window_rows = 2 * rows
    products = order * order * 3 // 4
    scratch = [
        pltpu.VMEM((ep_count, window_rows, LANES), F32),
        pltpu.VMEM((window_rows, span), BF16),
        pltpu.VMEM((window_rows, span), BF16),
        pltpu.VMEM((window_rows, span), BF16),
        pltpu.VMEM((window_rows, span), BF16),
        pltpu.VMEM((products, span), BF16),
        pltpu.VMEM((products, span), BF16),
        pltpu.VMEM((order, span), BF16),
        pltpu.VMEM((order, span), BF16),
        pltpu.VMEM((ep_count, LANES, LANES), BF16),
    ]
    args = (places, meta, win)
    everyone = ep_count * obj_count
    for iteration in range(ITERS):
        coef_t, send = call(
            make_step_kernel(iteration == 0),
            (shaped((order, window_rows)), shaped((8 * group, LANES))),
            args,
            scratch=scratch,
            scalar=True,
            name=f"objects_{iteration}",
        )
        arrived = lax.all_to_all(
            send.reshape(group, 8, LANES), "obj", split_axis=0, concat_axis=0, tiled=True
        )
        lines = call(
            lambda a, o: mode_kernel(a, o, order=order),
            shaped((everyone, 1, LANES)),
            (arrived,),
            name=f"modes_{iteration}",
        )
        if iteration == 0:
            lines, index = lax.optimization_barrier((lines, index))
        lines = lax.all_to_all(lines, ("ep", "obj"), split_axis=0, concat_axis=0, tiled=True)
        if iteration == 0:
            lines, *close = lax.optimization_barrier((lines, *basis_of(index, range(NEAR), False)))
            basis = close + basis
        args = (places, meta, win, lines.reshape(everyone, LANES), coef_t)
    basis[NEAR:] = [pltpu.with_memory_space_constraint(b, pltpu.HBM) for b in basis[NEAR:]]
    residual, power = call(
        lambda *refs: final_kernel(*refs, group=group),
        (shaped((rows, cols)), shaped((rows // ep_count, freq_index.shape[0]))),
        (*args, light_curves, *basis),
        scratch=[
            pltpu.VMEM((ep_count, rows, LANES), F32),
            pltpu.VMEM((2, rows, LANES), F32),
            pltpu.VMEM((2 * rows // ep_count, span), BF16),
            *[pltpu.VMEM((span, 2 * width), BF16) for _ in range(NEAR, CHUNKS)],
            pltpu.SemaphoreType.DMA((CHUNKS * PARTS,)),
        ],
        scalar=True,
        away=range(len(args) + 1 + NEAR, len(args) + 1 + CHUNKS),
        limit=32 << 20,
        name="spectrum",
    )
    return residual, power


def solution(mesh):
    in_specs = (P("obj", "ep"), P("obj", "ep"), P("obj"), P("obj"), P("ep", None), P(), P())
    out_specs = (P("obj", "ep"), P(("obj", "ep"), None))
    return jax.shard_map(
        per_device, mesh=mesh, in_specs=in_specs, out_specs=out_specs, check_vma=False
    )
```

```python
import jax
import jax.numpy as jnp
import numpy as np
from jax import lax
from jax.experimental import pallas as pl
from jax.experimental.pallas import tpu as pltpu
from jax.sharding import PartitionSpec as P

ITERS = 2
HUBER = 1.345
DAMP = 2.0
RIDGE = 0.05
INVALID = 1e9
F32 = jnp.float32
BF16 = jnp.bfloat16
LANES = 128
VMEM = 14 << 20
CHUNKS = 4
NEAR = 1
SLAB = 256
PARTS = 4
NEAREST = 1.5 * 2.0**23
NT = (((1,), (1,)), ((), ()))
NN = (((1,), (0,)), ((), ()))


def dot(a, b, dims):
    return lax.dot_general(a, b, dims, preferred_element_type=F32)


def split2(x):
    hi = x.astype(BF16)
    lo = (x - hi.astype(F32)).astype(BF16)
    return hi, lo


def split3(x):
    hi = x.astype(BF16).astype(F32)
    rest = x - hi
    mid = rest.astype(BF16).astype(F32)
    low = (rest - mid).astype(BF16).astype(F32)
    return hi, mid, low


def solve_columns(rows, target):
    order = len(rows)
    half = order // 2
    rows = list(rows)
    scaled = [None] * order
    forward = [None] * order
    for k in range(order):
        at = k if k < half else k - half
        row = rows[k]
        inverse = 1.0 / (row[at : at + 1] + DAMP)
        unit = row * inverse
        scaled[k] = unit
        value = target[k : k + 1] * inverse
        forward[k] = value
        for i in range(k + 1, order):
            here = i if k < half else i - half
            factor = row[here : here + 1]
            if i >= half and k < half:
                rows[i] = rows[i] - factor * unit[half:]
            else:
                rows[i] = rows[i] - factor * unit
        if k < half:
            target = target - row * value
        else:
            target = jnp.concatenate([target[:half], target[half:] - row * value], axis=0)
    width = target.shape[1]
    level = lax.broadcasted_iota(jnp.int32, (half, width), 0)
    upper = jnp.zeros((half, width), F32)
    lower = jnp.zeros((half, width), F32)
    for k in reversed(range(order)):
        unit = scaled[k]
        if k >= half:
            value = forward[k] - jnp.sum(unit * lower, axis=0, keepdims=True)
            lower = jnp.where(level == k - half, value, lower)
        else:
            both = unit[:half] * upper + unit[half:] * lower
            value = forward[k] - jnp.sum(both, axis=0, keepdims=True)
            upper = jnp.where(level == k, value, upper)
    return jnp.concatenate([upper, lower], axis=0)


def outer_rows(x):
    half = x.shape[0] // 2
    upper = [x[i : i + 1] * x for i in range(half)]
    lower = [x[i : i + 1] * x[half:] for i in range(half, 2 * half)]
    return jnp.concatenate(upper + lower, axis=0)


def rows_of(gram, order):
    half = order // 2
    top = [gram[order * i : order * (i + 1)] for i in range(half)]
    start = order * half
    return top + [gram[start + half * i : start + half * (i + 1)] for i in range(half)]


def coef_factors(coef_t):
    order = coef_t.shape[0]
    hi, mid, low = split3(coef_t)
    none = jnp.zeros((LANES - 6 * order, coef_t.shape[1]), F32)
    stack = jnp.concatenate([hi, mid, low, hi, mid, hi, none], axis=0)
    return stack.T.astype(BF16)


def mode_factors(modes_b):
    order = modes_b.shape[0]
    hi, mid, low = split3(modes_b)
    none = jnp.zeros((LANES - 6 * order, modes_b.shape[1]), F32)
    return jnp.concatenate([hi, hi, hi, mid, mid, low, none], axis=0).astype(BF16)


def window(meta):
    rows = meta.shape[1]
    filled = jnp.concatenate([meta, jnp.zeros((LANES - meta.shape[0], rows), F32)], axis=0)
    turned = filled.T
    same = (turned[:, 0:1] == meta[0:1]).astype(F32).astype(BF16)
    return same, turned[:, 1:2]


def own_of(win_ref, b, rows):
    coded = win_ref[b, :rows].astype(F32) + win_ref[b, rows : 2 * rows].astype(F32)
    ok = coded < 0.5 * INVALID
    return ok, jnp.where(ok, coded, 0.0)


def block_of(win_ref, b, rows):
    own = win_ref[b, :rows].astype(F32) + win_ref[b, rows : 2 * rows].astype(F32)
    coded = jnp.concatenate([own, win_ref[b, 2 * rows : 3 * rows].astype(F32)], axis=0)
    ok = coded < 0.5 * INVALID
    return ok, jnp.where(ok, coded, 0.0)


def first_modes(win_ref, b, rows, order):
    parts = win_ref[b, 3 * rows :].astype(F32)
    return parts[:order] + (parts[order : 2 * order] + parts[2 * order :])


def pixel_total(same, part):
    hi, mid, low = split3(part)
    wide = jnp.concatenate([hi, mid, low], axis=1).astype(BF16)
    total = dot(same, wide, NN)
    total = total[:, :LANES] + total[:, LANES : 2 * LANES] + total[:, 2 * LANES :]
    return jnp.sum(total, axis=1, keepdims=True)


def spread_of(same, part, count):
    return jnp.sqrt(pixel_total(same, part) / jnp.maximum(count, 1.0) + 1e-06)


def robust_weight(ok, scaled, edge, sigma):
    return jnp.where(ok, (sigma * sigma) * (edge / jnp.maximum(jnp.abs(scaled), edge)), 0.0)


def natural_modes(arrived, blocks, group, order):
    turns = LANES // group
    lane = lax.broadcasted_iota(jnp.int32, (order, LANES), 1)
    turned = arrived.T
    out = []
    for b in range(blocks):
        tile, inner = divmod(b * group, LANES)
        total = jnp.zeros((order, LANES), F32)
        for r in range(turns):
            piece = turned[order * r : order * (r + 1), LANES * tile : LANES * (tile + 1)]
            shift = (group * r - inner) % LANES
            if shift:
                piece = pltpu.roll(piece, shift, 1)
            inside = (lane >= group * r) & (lane < group * (r + 1))
            total = jnp.where(inside, piece, total)
        out.append(total)
    return out


def prep_kernel(lc_hbm, valid_hbm, pix_hbm, sig_hbm, init_hbm, own_ref, tail_ref, head_ref,
                lc_ref, valid_ref, pix_ref, sig_ref, init_ref, sems):
    pairs = (
        (lc_hbm, lc_ref), (valid_hbm, valid_ref), (pix_hbm, pix_ref), (sig_hbm, sig_ref), (init_hbm, init_ref)
    )
    copies = [pltpu.make_async_copy(a, b, sems.at[i]) for i, (a, b) in enumerate(pairs)]
    for copy in copies:
        copy.start()
    for copy in copies:
        copy.wait()
    rows = lc_ref.shape[0]
    half = rows // 2
    coded = jnp.where(valid_ref[...] != 0, lc_ref[...], INVALID)
    own_ref[:rows], own_ref[rows : 2 * rows] = split2(coded)
    own_ref[2 * rows :] = jnp.concatenate(split3(init_ref[...]), axis=0).astype(BF16)
    meta = jnp.concatenate(
        [pix_ref[...].astype(F32), sig_ref[...], jnp.zeros((6, rows), F32)], axis=0
    )
    tail_ref[:half] = coded[half:]
    tail_ref[half:] = meta
    head_ref[:half] = coded[:half]
    head_ref[half:] = meta


def widen_kernel(own_ref, tail_ref, left_ref, right_ref, out_hbm, meta_ref, one_ref, sems):
    rows = tail_ref.shape[1]
    half = rows // 2
    left = left_ref[...]
    right = right_ref[...]
    one_ref[: 2 * rows] = own_ref[: 2 * rows]
    one_ref[2 * rows : 3 * rows] = jnp.concatenate([left[:half], right[:half]], axis=0).astype(BF16)
    one_ref[3 * rows :] = own_ref[2 * rows :]
    copies = [pltpu.make_async_copy(one_ref, out_hbm.at[b], sems.at[b]) for b in range(out_hbm.shape[0])]
    for copy in copies:
        copy.start()
    lane = lax.broadcasted_iota(jnp.int32, (8, rows), 1)
    beyond = pltpu.roll(jnp.where(lane >= half, left[half:], right[half:]), half, 1)
    meta_ref[:, :rows] = tail_ref[half:]
    meta_ref[:, rows:] = beyond
    for copy in copies:
        copy.wait()


def make_step_kernel(first):
    def kernel(*refs):
        if first:
            place_ref, meta_ref, win_ref = refs[:3]
            rest = refs[3:]
        else:
            place_ref, meta_ref, win_ref, arrived_ref, before_ref = refs[:5]
            rest = refs[5:]
        coef_ref, send_ref, scal_ref, wh_ref, wl_ref, ph_ref, pl_ref, oh_ref, ol_ref, mh_ref, ml_ref, ms_ref = rest
        blocks = win_ref.shape[0]
        order = coef_ref.shape[0]
        rows = meta_ref.shape[1]
        own_rows = rows // 2
        group = send_ref.shape[0] // 8
        same, sigma = window(meta_ref[...])
        if first:
            modes = [first_modes(win_ref, b, own_rows, order) for b in range(blocks)]
        else:
            modes = natural_modes(arrived_ref[...], blocks, group, order)
            factors = coef_factors(before_ref[...])
        part = jnp.zeros((rows, LANES), F32)
        seen = jnp.zeros((rows, LANES), F32)
        for b in range(blocks):
            ok, lc = block_of(win_ref, b, own_rows)
            ms_ref[b] = mode_factors(modes[b])
            if not first:
                lc = lc - dot(factors, ms_ref[b], NN)
            scaled = lc * sigma
            scal_ref[b] = scaled
            part = part + jnp.where(ok, scaled * scaled, 0.0)
            seen = seen + jnp.where(ok, 1.0, 0.0)
        count = jnp.sum(dot(same, seen.astype(BF16), NN), axis=1, keepdims=True)
        edge = HUBER * spread_of(same, part, count)
        for b in range(blocks):
            ok, lc = block_of(win_ref, b, own_rows)
            weight = robust_weight(ok, scal_ref[b], edge, sigma)
            at = slice(LANES * b, LANES * (b + 1))
            wh_ref[:, at], wl_ref[:, at] = split2(weight)
            ph_ref[:, at], pl_ref[:, at] = split2(weight * lc)
            oh_ref[:, at], ol_ref[:, at] = split2(outer_rows(modes[b]))
            mh_ref[:, at], ml_ref[:, at] = split2(modes[b])
        gram = (
            dot(oh_ref[...], wh_ref[...], NT)
            + dot(oh_ref[...], wl_ref[...], NT)
            + dot(ol_ref[...], wh_ref[...], NT)
        )
        target = (
            dot(mh_ref[...], ph_ref[...], NT)
            + dot(mh_ref[...], pl_ref[...], NT)
            + dot(ml_ref[...], ph_ref[...], NT)
        )
        coef_t = solve_columns(rows_of(gram, order), target)
        coef_ref[...] = coef_t
        factors = coef_factors(coef_t)
        part = jnp.zeros((rows, LANES), F32)
        for b in range(blocks):
            ok, lc = block_of(win_ref, b, own_rows)
            scaled = (lc - dot(factors, ms_ref[b], NN)) * sigma
            scal_ref[b] = scaled
            part = part + jnp.where(ok, scaled * scaled, 0.0)
        edge = HUBER * spread_of(same, part, count)
        place = place_ref[0]
        ok, lc = own_of(win_ref, place, own_rows)
        weight = robust_weight(ok, scal_ref[place, :own_rows], edge[:own_rows], sigma[:own_rows])
        weight_hi, weight_lo = split2(weight)
        value_hi, value_lo = split2(weight * lc)
        own_coef = coef_t[:, :own_rows]
        outer_hi, outer_lo = split2(outer_rows(own_coef))
        coef_hi, coef_lo = split2(own_coef)
        gram = dot(outer_hi, weight_hi, NN) + dot(outer_hi, weight_lo, NN) + dot(outer_lo, weight_hi, NN)
        target = dot(coef_hi, value_hi, NN) + dot(coef_hi, value_lo, NN) + dot(coef_lo, value_hi, NN)
        spare = jnp.zeros((2 * LANES - gram.shape[0] - order, LANES), F32)
        tall = jnp.concatenate([gram, target, spare], axis=0)
        turns = LANES // group
        for side in range(2):
            turned = tall[LANES * side : LANES * (side + 1)].T
            for r in range(turns):
                send_ref[pl.ds(turns * side + r, group, stride=8), :] = turned[group * r : group * (r + 1)]

    return kernel


def mode_kernel(arrived_ref, out_ref, *, order):
    total = arrived_ref[0]
    for j in range(1, arrived_ref.shape[0]):
        total = total + arrived_ref[j]
    turns = total.shape[0] // 2
    tall = jnp.concatenate([total, jnp.zeros((LANES - 2 * turns, LANES), F32)], axis=0).T
    after = pltpu.roll(tall, LANES - turns, 1)
    half = order // 2
    gram = jnp.concatenate([tall, after[: half * half]], axis=0)
    target = after[half * half : half * half + order]
    solved = solve_columns(rows_of(gram, order), target)
    lane = lax.broadcasted_iota(jnp.int32, solved.shape, 1)
    solved = jnp.where(lane < turns, solved, 0.0)
    wide = jnp.concatenate([solved, jnp.zeros((LANES - order, LANES), F32)], axis=0).T
    line = wide[0:1]
    for r in range(1, turns):
        line = line + pltpu.roll(wide[0:8], order * r, 1)[r : r + 1]
    out_ref[...] = jnp.broadcast_to(line.reshape(1, 1, LANES), out_ref.shape)


def half_turn_series():
    grid = (np.cos(np.pi * (np.arange(400) + 0.5) / 400) + 1) / 2
    u = np.sqrt(grid) / 2
    sine = np.polynomial.polynomial.polyfit(grid, np.sin(np.pi * u) / u, 4)
    cosine = np.polynomial.polynomial.polyfit(grid, np.cos(np.pi * u), 5)
    return [float(c) * 4.0**k for k, c in enumerate(sine)], [float(c) * 4.0**k for k, c in enumerate(cosine)]


SINE, COSINE = half_turn_series()


def horner(series, x):
    total = x * series[-1] + series[-2]
    for c in series[-3::-1]:
        total = total * x + c
    return total


def basis_kernel(jitter_ref, index_ref, *rest, pieces, far):
    count = len(pieces)
    time_ref = rest[count]
    made = rest[count + 1 : 2 * count + 1] if far else rest[:count]
    blocks, width = jitter_ref.shape[0], made[0].shape[1] // 2
    tiles = width // LANES
    freqs = (index_ref[...] + 1).astype(F32) / (4.0 * time_ref.shape[0])
    jitter = jnp.concatenate([jitter_ref[...], jnp.zeros((LANES - blocks, LANES), F32)], axis=0).T
    index = lax.broadcasted_iota(jnp.int32, (LANES, LANES), 0)
    for b in range(blocks):
        time_ref[LANES * b : LANES * (b + 1)] = (index + LANES * b).astype(F32) + jitter[:, b : b + 1]
    step = 32

    def copy(c, b):
        at = pl.ds(pl.multiple_of(LANES * b, LANES), LANES)
        return pltpu.make_async_copy(made[c].at[at], rest[c].at[at], rest[-1].at[c, b])

    @pl.loop(0, blocks)
    def _(b):
        @pl.loop(0, LANES // step)
        def _(i):
            at = pl.ds(pl.multiple_of(LANES * b + step * i, step), step)
            times = time_ref[at]
            for c in range(count):
                for n in range(tiles):
                    line = pieces[c] * tiles + n
                    cycles = times * freqs[line : line + 1]
                    turn = cycles - ((cycles + NEAREST) - NEAREST)
                    square = turn * turn
                    sine = turn * horner(SINE, square)
                    cosine = horner(COSINE, square)
                    twice = sine + sine
                    start = LANES * n
                    made[c][at, start : start + LANES] = (1.0 - twice * sine).astype(BF16)
                    made[c][at, start + width : start + width + LANES] = (twice * cosine).astype(BF16)

        if far:
            for c in range(count):
                copy(c, b).start()

    if far:

        @pl.loop(0, blocks)
        def _(b):
            for c in range(count):
                copy(c, b).wait()


def final_kernel(place_ref, meta_ref, win_ref, arrived_ref, coef_ref, lc_ref, *rest, group):
    far, (resid_ref, power_ref, res_ref, col_ref, both_ref) = rest[:CHUNKS], rest[CHUNKS : CHUNKS + 5]
    basis_refs, sems = far[:NEAR] + rest[CHUNKS + 5 : -1], rest[-1]
    copies = [None] * (PARTS * NEAR)
    for c in range(NEAR, CHUNKS):
        tall = basis_refs[c].shape[0] // PARTS
        for k in range(PARTS):
            at = pl.ds(tall * k, tall)
            copies.append(pltpu.make_async_copy(far[c].at[at], basis_refs[c].at[at], sems.at[c * PARTS + k]))
            copies[-1].start()
    blocks = win_ref.shape[0]
    order = coef_ref.shape[0]
    rows = meta_ref.shape[1]
    own_rows = rows // 2
    share = power_ref.shape[0]
    same, sigma = window(meta_ref[...])
    modes = natural_modes(arrived_ref[...], blocks, group, order)
    factors = coef_factors(coef_ref[...])
    part = jnp.zeros((rows, LANES), F32)
    seen = jnp.zeros((rows, LANES), F32)
    for b in range(blocks):
        ok, lc = block_of(win_ref, b, own_rows)
        resid = lc - dot(factors, mode_factors(modes[b]), NN)
        res_ref[b] = resid[:own_rows]
        scaled = resid * sigma
        part = part + jnp.where(ok, scaled * scaled, 0.0)
        seen = seen + jnp.where(ok, 1.0, 0.0)
    count = jnp.sum(dot(same, seen.astype(BF16), NN), axis=1, keepdims=True)
    edge = HUBER * spread_of(same, part, count)
    col_ref[0] = jnp.broadcast_to(edge[:own_rows], (own_rows, LANES))
    col_ref[1] = jnp.broadcast_to(sigma[:own_rows], (own_rows, LANES))
    place = place_ref[0]
    ok, lc = own_of(win_ref, place, own_rows)
    resid_ref[...] = lc_ref[...] - (lc - res_ref[place])
    mine = pl.ds(pl.multiple_of(place * share, share), share)
    edge = col_ref[0, mine]
    sigma = col_ref[1, mine]
    total = jnp.zeros((share, LANES), F32)
    level = jnp.zeros((share, LANES), F32)
    for b in range(blocks):
        ok = win_ref[b, mine].astype(F32) < 0.5 * INVALID
        resid = res_ref[b, mine]
        weight = robust_weight(ok, resid * sigma, edge, sigma)
        at = slice(LANES * b, LANES * (b + 1))
        weight_b = weight.astype(BF16)
        value_b = (weight * resid).astype(BF16)
        both_ref[:share, at] = weight_b
        both_ref[share:, at] = value_b
        total = total + weight_b.astype(F32)
        level = level + value_b.astype(F32)
    total = jnp.sum(total, axis=1, keepdims=True)
    level = jnp.sum(level, axis=1, keepdims=True)
    inverse = 1.0 / total
    mean_level = level * inverse
    for c, basis_ref in enumerate(basis_refs):
        width = basis_ref.shape[1] // 2
        for copy in copies[PARTS * c : PARTS * (c + 1)] if c >= NEAR else ():
            copy.wait()
        single = jnp.zeros((2 * share, 2 * width), F32)
        double_cos = [jnp.zeros((share, SLAB), F32) for _ in range(width // SLAB)]
        double_sin = [jnp.zeros((share, SLAB), F32) for _ in range(width // SLAB)]
        for k in range(basis_ref.shape[0] // SLAB):
            at = slice(SLAB * k, SLAB * (k + 1))
            single = single + dot(both_ref[:, at], basis_ref[at], NN)
            for n in range(width // SLAB):
                cos_b = basis_ref[at, SLAB * n : SLAB * (n + 1)]
                sin_b = basis_ref[at, width + SLAB * n : width + SLAB * (n + 1)]
                twice = sin_b + sin_b
                cos_two = 1.0 - twice * sin_b
                sin_two = twice * cos_b
                double_cos[n] = double_cos[n] + dot(both_ref[:share, at], cos_two, NN)
                double_sin[n] = double_sin[n] + dot(both_ref[:share, at], sin_two, NN)
        cosine = single[:share, :width]
        sine = single[:share, width:]
        cosine_two = jnp.concatenate(double_cos, axis=1)
        sine_two = jnp.concatenate(double_sin, axis=1)
        ycos = single[share:, :width] - mean_level * cosine
        ysin = single[share:, width:] - mean_level * sine
        cc_term = 0.5 * (total + cosine_two) - cosine * cosine * inverse + RIDGE * total
        ss_term = 0.5 * (total - cosine_two) - sine * sine * inverse + RIDGE * total
        cs_term = 0.5 * sine_two - cosine * sine * inverse
        determinant = cc_term * ss_term - cs_term * cs_term
        power = (ss_term * ycos * ycos + cc_term * ysin * ysin - 2.0 * cs_term * ycos * ysin) / determinant
        power_ref[:, width * c : width * (c + 1)] = power


def shaped(shape, dtype=F32):
    return jax.ShapeDtypeStruct(shape, dtype)


def call(kernel, out_shape, args, scratch=(), scalar=False, away=(), out_space=pltpu.VMEM, limit=VMEM, name=None):
    specs = [pl.BlockSpec(memory_space=pltpu.HBM if at in away else pltpu.VMEM) for at in range(len(args))]
    if scalar:
        specs[0] = pl.BlockSpec(memory_space=pltpu.SMEM)
    many = isinstance(out_shape, (tuple, list))
    spaces = out_space if isinstance(out_space, (tuple, list)) else [out_space] * (len(out_shape) if many else 1)
    out_specs = [pl.BlockSpec(memory_space=space) for space in spaces]
    return pl.pallas_call(
        kernel,
        out_shape=out_shape,
        in_specs=specs,
        out_specs=out_specs if many else out_specs[0],
        scratch_shapes=list(scratch),
        compiler_params=pltpu.CompilerParams(vmem_limit_bytes=limit),
        name=name,
    )(*args)


def per_device(light_curves, valid, pixel, inv_sigma, modes_init, epoch_jitter, freq_index):
    obj_count = lax.axis_size("obj")
    ep_count = lax.axis_size("ep")
    rows, cols = light_curves.shape
    order = modes_init.shape[1]
    half = rows // 2
    span = ep_count * cols
    group = obj_count
    place = lax.axis_index("ep").astype(jnp.int32)
    places = place.reshape(1)

    fetched = (light_curves, valid, pixel.reshape(1, rows), inv_sigma.reshape(1, rows), modes_init.T)
    fetched = tuple(pltpu.with_memory_space_constraint(a, pltpu.HBM) for a in fetched)
    own, tail, head = call(
        prep_kernel,
        (shaped((2 * rows + 3 * order, cols), BF16), shaped((half + 8, cols)), shaped((half + 8, cols))),
        fetched,
        scratch=[pltpu.VMEM(a.shape, a.dtype) for a in fetched] + [pltpu.SemaphoreType.DMA((5,))],
        away=range(5),
        name="prep",
    )
    ring = [(i, (i + 1) % obj_count) for i in range(obj_count)]
    back = [(i, (i - 1) % obj_count) for i in range(obj_count)]
    left = lax.ppermute(tail, "obj", ring)
    right = lax.ppermute(head, "obj", back)
    shape = (ep_count, 3 * (rows + order), cols)
    wide, meta = call(
        widen_kernel,
        (pltpu.HBM(shape, BF16), shaped((8, 2 * rows))),
        (own, tail, left, right),
        scratch=[pltpu.VMEM(shape[1:], BF16), pltpu.SemaphoreType.DMA((ep_count,))],
        out_space=(pltpu.HBM, pltpu.VMEM),
        name="widen",
    )

    width = freq_index.shape[0] // CHUNKS
    jitter = epoch_jitter.reshape(ep_count, cols)

    index = freq_index.reshape(-1, LANES)

    def basis_of(index, pieces, far):
        scratch = [pltpu.VMEM((span, LANES), F32)]
        if far:
            scratch += [pltpu.VMEM((span, 2 * width), BF16) for _ in pieces]
            scratch += [pltpu.SemaphoreType.DMA((len(pieces), ep_count))]
        place_of = pltpu.HBM if far else shaped
        return call(
            lambda *refs: basis_kernel(*refs, pieces=pieces, far=far),
            [place_of((span, 2 * width), BF16) for _ in pieces],
            (jitter, index),
            scratch=scratch,
            out_space=[pltpu.HBM if far else pltpu.VMEM] * len(pieces),
            name="basis",
        )

    wide, index = lax.optimization_barrier((wide, index))
    win = lax.all_to_all(wide, "ep", split_axis=0, concat_axis=0, tiled=True)
    win, *basis = lax.optimization_barrier((win, *basis_of(index, range(NEAR, CHUNKS), True)))

    window_rows = 2 * rows
    products = order * order * 3 // 4
    scratch = [
        pltpu.VMEM((ep_count, window_rows, LANES), F32),
        pltpu.VMEM((window_rows, span), BF16),
        pltpu.VMEM((window_rows, span), BF16),
        pltpu.VMEM((window_rows, span), BF16),
        pltpu.VMEM((window_rows, span), BF16),
        pltpu.VMEM((products, span), BF16),
        pltpu.VMEM((products, span), BF16),
        pltpu.VMEM((order, span), BF16),
        pltpu.VMEM((order, span), BF16),
        pltpu.VMEM((ep_count, LANES, LANES), BF16),
    ]
    args = (places, meta, win)
    everyone = ep_count * obj_count
    for iteration in range(ITERS):
        coef_t, send = call(
            make_step_kernel(iteration == 0),
            (shaped((order, window_rows)), shaped((8 * group, LANES))),
            args,
            scratch=scratch,
            scalar=True,
            name=f"objects_{iteration}",
        )
        arrived = lax.all_to_all(
            send.reshape(group, 8, LANES), "obj", split_axis=0, concat_axis=0, tiled=True
        )
        lines = call(
            lambda a, o: mode_kernel(a, o, order=order),
            shaped((everyone, 1, LANES)),
            (arrived,),
            name=f"modes_{iteration}",
        )
        if iteration == 0:
            lines, index = lax.optimization_barrier((lines, index))
        lines = lax.all_to_all(lines, ("ep", "obj"), split_axis=0, concat_axis=0, tiled=True)
        if iteration == 0:
            lines, *close = lax.optimization_barrier((lines, *basis_of(index, range(NEAR), False)))
            basis = close + basis
        args = (places, meta, win, lines.reshape(everyone, LANES), coef_t)
    basis[NEAR:] = [pltpu.with_memory_space_constraint(b, pltpu.HBM) for b in basis[NEAR:]]
    residual, power = call(
        lambda *refs: final_kernel(*refs, group=group),
        (shaped((rows, cols)), shaped((rows // ep_count, freq_index.shape[0]))),
        (*args, light_curves, *basis),
        scratch=[
            pltpu.VMEM((ep_count, rows, LANES), F32),
            pltpu.VMEM((2, rows, LANES), F32),
            pltpu.VMEM((2 * rows // ep_count, span), BF16),
            *[pltpu.VMEM((span, 2 * width), BF16) for _ in range(NEAR, CHUNKS)],
            pltpu.SemaphoreType.DMA((CHUNKS * PARTS,)),
        ],
        scalar=True,
        away=range(len(args) + 1 + NEAR, len(args) + 1 + CHUNKS),
        limit=32 << 20,
        name="spectrum",
    )
    return residual, power


def solution(mesh):
    in_specs = (P("obj", "ep"), P("obj", "ep"), P("obj"), P("obj"), P("ep", None), P(), P())
    out_specs = (P("obj", "ep"), P(("obj", "ep"), None))
    return jax.shard_map(
        per_device, mesh=mesh, in_specs=in_specs, out_specs=out_specs, check_vma=False
    )
```

```python
import jax
import jax.numpy as jnp
import numpy as np
from jax import lax
from jax.experimental import pallas as pl
from jax.experimental.pallas import tpu as pltpu
from jax.sharding import PartitionSpec as P

ITERS = 2
HUBER = 1.345
DAMP = 2.0
RIDGE = 0.05
INVALID = 1e9
F32 = jnp.float32
BF16 = jnp.bfloat16
LANES = 128
VMEM = 14 << 20
CHUNKS = 4
NEAR = 1
SLAB = 256
PARTS = 4
NEAREST = 1.5 * 2.0**23
NT = (((1,), (1,)), ((), ()))
NN = (((1,), (0,)), ((), ()))


def dot(a, b, dims):
    return lax.dot_general(a, b, dims, preferred_element_type=F32)


def split2(x):
    hi = x.astype(BF16)
    lo = (x - hi.astype(F32)).astype(BF16)
    return hi, lo


def split3(x):
    hi = x.astype(BF16).astype(F32)
    rest = x - hi
    mid = rest.astype(BF16).astype(F32)
    low = (rest - mid).astype(BF16).astype(F32)
    return hi, mid, low


def solve_columns(rows, target):
    order = len(rows)
    half = order // 2
    rows = list(rows)
    scaled = [None] * order
    forward = [None] * order
    for k in range(order):
        at = k if k < half else k - half
        row = rows[k]
        inverse = 1.0 / (row[at : at + 1] + DAMP)
        unit = row * inverse
        scaled[k] = unit
        value = target[k : k + 1] * inverse
        forward[k] = value
        for i in range(k + 1, order):
            here = i if k < half else i - half
            factor = row[here : here + 1]
            if i >= half and k < half:
                rows[i] = rows[i] - factor * unit[half:]
            else:
                rows[i] = rows[i] - factor * unit
        if k < half:
            target = target - row * value
        else:
            target = jnp.concatenate([target[:half], target[half:] - row * value], axis=0)
    width = target.shape[1]
    level = lax.broadcasted_iota(jnp.int32, (half, width), 0)
    upper = jnp.zeros((half, width), F32)
    lower = jnp.zeros((half, width), F32)
    for k in reversed(range(order)):
        unit = scaled[k]
        if k >= half:
            value = forward[k] - jnp.sum(unit * lower, axis=0, keepdims=True)
            lower = jnp.where(level == k - half, value, lower)
        else:
            both = unit[:half] * upper + unit[half:] * lower
            value = forward[k] - jnp.sum(both, axis=0, keepdims=True)
            upper = jnp.where(level == k, value, upper)
    return jnp.concatenate([upper, lower], axis=0)


def outer_rows(x):
    half = x.shape[0] // 2
    upper = [x[i : i + 1] * x for i in range(half)]
    lower = [x[i : i + 1] * x[half:] for i in range(half, 2 * half)]
    return jnp.concatenate(upper + lower, axis=0)


def rows_of(gram, order):
    half = order // 2
    top = [gram[order * i : order * (i + 1)] for i in range(half)]
    start = order * half
    return top + [gram[start + half * i : start + half * (i + 1)] for i in range(half)]


def coef_factors(coef_t):
    order = coef_t.shape[0]
    hi, mid, low = split3(coef_t)
    none = jnp.zeros((LANES - 6 * order, coef_t.shape[1]), F32)
    stack = jnp.concatenate([hi, mid, low, hi, mid, hi, none], axis=0)
    return stack.T.astype(BF16)


def mode_factors(modes_b):
    order = modes_b.shape[0]
    hi, mid, low = split3(modes_b)
    none = jnp.zeros((LANES - 6 * order, modes_b.shape[1]), F32)
    return jnp.concatenate([hi, hi, hi, mid, mid, low, none], axis=0).astype(BF16)


def window(meta):
    rows = meta.shape[1]
    filled = jnp.concatenate([meta, jnp.zeros((LANES - meta.shape[0], rows), F32)], axis=0)
    turned = filled.T
    same = (turned[:, 0:1] == meta[0:1]).astype(F32).astype(BF16)
    return same, turned[:, 1:2]


def own_of(win_ref, b, rows):
    coded = win_ref[b, :rows].astype(F32) + win_ref[b, rows : 2 * rows].astype(F32)
    ok = coded < 0.5 * INVALID
    return ok, jnp.where(ok, coded, 0.0)


def block_of(win_ref, b, rows):
    own = win_ref[b, :rows].astype(F32) + win_ref[b, rows : 2 * rows].astype(F32)
    coded = jnp.concatenate([own, win_ref[b, 2 * rows : 3 * rows].astype(F32)], axis=0)
    ok = coded < 0.5 * INVALID
    return ok, jnp.where(ok, coded, 0.0)


def first_modes(win_ref, b, rows, order):
    parts = win_ref[b, 3 * rows :].astype(F32)
    return parts[:order] + (parts[order : 2 * order] + parts[2 * order :])


def pixel_total(same, part):
    hi, mid, low = split3(part)
    wide = jnp.concatenate([hi, mid, low], axis=1).astype(BF16)
    total = dot(same, wide, NN)
    total = total[:, :LANES] + total[:, LANES : 2 * LANES] + total[:, 2 * LANES :]
    return jnp.sum(total, axis=1, keepdims=True)


def spread_of(same, part, count):
    return jnp.sqrt(pixel_total(same, part) / jnp.maximum(count, 1.0) + 1e-06)


def robust_weight(ok, scaled, edge, sigma):
    return jnp.where(ok, (sigma * sigma) * (edge / jnp.maximum(jnp.abs(scaled), edge)), 0.0)


def natural_modes(arrived, blocks, group, order):
    turns = LANES // group
    lane = lax.broadcasted_iota(jnp.int32, (order, LANES), 1)
    turned = arrived.T
    out = []
    for b in range(blocks):
        tile, inner = divmod(b * group, LANES)
        total = jnp.zeros((order, LANES), F32)
        for r in range(turns):
            piece = turned[order * r : order * (r + 1), LANES * tile : LANES * (tile + 1)]
            shift = (group * r - inner) % LANES
            if shift:
                piece = pltpu.roll(piece, shift, 1)
            inside = (lane >= group * r) & (lane < group * (r + 1))
            total = jnp.where(inside, piece, total)
        out.append(total)
    return out


def prep_kernel(lc_hbm, valid_hbm, pix_hbm, sig_hbm, init_hbm, own_ref, tail_ref, head_ref,
                lc_ref, valid_ref, pix_ref, sig_ref, init_ref, sems):
    pairs = (
        (lc_hbm, lc_ref), (valid_hbm, valid_ref), (pix_hbm, pix_ref), (sig_hbm, sig_ref), (init_hbm, init_ref)
    )
    copies = [pltpu.make_async_copy(a, b, sems.at[i]) for i, (a, b) in enumerate(pairs)]
    for copy in copies:
        copy.start()
    for copy in copies:
        copy.wait()
    rows = lc_ref.shape[0]
    half = rows // 2
    coded = jnp.where(valid_ref[...] != 0, lc_ref[...], INVALID)
    own_ref[:rows], own_ref[rows : 2 * rows] = split2(coded)
    own_ref[2 * rows :] = jnp.concatenate(split3(init_ref[...]), axis=0).astype(BF16)
    meta = jnp.concatenate(
        [pix_ref[...].astype(F32), sig_ref[...], jnp.zeros((6, rows), F32)], axis=0
    )
    tail_ref[:half] = coded[half:]
    tail_ref[half:] = meta
    head_ref[:half] = coded[:half]
    head_ref[half:] = meta


def widen_kernel(own_ref, tail_ref, left_ref, right_ref, out_hbm, meta_ref, one_ref, sems):
    rows = tail_ref.shape[1]
    half = rows // 2
    left = left_ref[...]
    right = right_ref[...]
    one_ref[: 2 * rows] = own_ref[: 2 * rows]
    one_ref[2 * rows : 3 * rows] = jnp.concatenate([left[:half], right[:half]], axis=0).astype(BF16)
    one_ref[3 * rows :] = own_ref[2 * rows :]
    copies = [pltpu.make_async_copy(one_ref, out_hbm.at[b], sems.at[b]) for b in range(out_hbm.shape[0])]
    for copy in copies:
        copy.start()
    lane = lax.broadcasted_iota(jnp.int32, (8, rows), 1)
    beyond = pltpu.roll(jnp.where(lane >= half, left[half:], right[half:]), half, 1)
    meta_ref[:, :rows] = tail_ref[half:]
    meta_ref[:, rows:] = beyond
    for copy in copies:
        copy.wait()


def make_step_kernel(first):
    def kernel(*refs):
        if first:
            place_ref, meta_ref, win_ref = refs[:3]
            rest = refs[3:]
        else:
            place_ref, meta_ref, win_ref, arrived_ref, before_ref = refs[:5]
            rest = refs[5:]
        coef_ref, send_ref, scal_ref, wh_ref, wl_ref, ph_ref, pl_ref, oh_ref, ol_ref, mh_ref, ml_ref, ms_ref = rest
        blocks = win_ref.shape[0]
        order = coef_ref.shape[0]
        rows = meta_ref.shape[1]
        own_rows = rows // 2
        group = send_ref.shape[0] // 8
        same, sigma = window(meta_ref[...])
        if first:
            modes = [first_modes(win_ref, b, own_rows, order) for b in range(blocks)]
        else:
            modes = natural_modes(arrived_ref[...], blocks, group, order)
            factors = coef_factors(before_ref[...])
        part = jnp.zeros((rows, LANES), F32)
        seen = jnp.zeros((rows, LANES), F32)
        for b in range(blocks):
            ok, lc = block_of(win_ref, b, own_rows)
            ms_ref[b] = mode_factors(modes[b])
            if not first:
                lc = lc - dot(factors, ms_ref[b], NN)
            scaled = lc * sigma
            scal_ref[b] = scaled
            part = part + jnp.where(ok, scaled * scaled, 0.0)
            seen = seen + jnp.where(ok, 1.0, 0.0)
        count = jnp.sum(dot(same, seen.astype(BF16), NN), axis=1, keepdims=True)
        edge = HUBER * spread_of(same, part, count)
        for b in range(blocks):
            ok, lc = block_of(win_ref, b, own_rows)
            weight = robust_weight(ok, scal_ref[b], edge, sigma)
            at = slice(LANES * b, LANES * (b + 1))
            wh_ref[:, at], wl_ref[:, at] = split2(weight)
            ph_ref[:, at], pl_ref[:, at] = split2(weight * lc)
            oh_ref[:, at], ol_ref[:, at] = split2(outer_rows(modes[b]))
            mh_ref[:, at], ml_ref[:, at] = split2(modes[b])
        gram = (
            dot(oh_ref[...], wh_ref[...], NT)
            + dot(oh_ref[...], wl_ref[...], NT)
            + dot(ol_ref[...], wh_ref[...], NT)
        )
        target = (
            dot(mh_ref[...], ph_ref[...], NT)
            + dot(mh_ref[...], pl_ref[...], NT)
            + dot(ml_ref[...], ph_ref[...], NT)
        )
        coef_t = solve_columns(rows_of(gram, order), target)
        coef_ref[...] = coef_t
        factors = coef_factors(coef_t)
        part = jnp.zeros((rows, LANES), F32)
        for b in range(blocks):
            ok, lc = block_of(win_ref, b, own_rows)
            scaled = (lc - dot(factors, ms_ref[b], NN)) * sigma
            scal_ref[b] = scaled
            part = part + jnp.where(ok, scaled * scaled, 0.0)
        edge = HUBER * spread_of(same, part, count)
        place = place_ref[0]
        ok, lc = own_of(win_ref, place, own_rows)
        weight = robust_weight(ok, scal_ref[place, :own_rows], edge[:own_rows], sigma[:own_rows])
        weight_hi, weight_lo = split2(weight)
        value_hi, value_lo = split2(weight * lc)
        own_coef = coef_t[:, :own_rows]
        outer_hi, outer_lo = split2(outer_rows(own_coef))
        coef_hi, coef_lo = split2(own_coef)
        gram = dot(outer_hi, weight_hi, NN) + dot(outer_hi, weight_lo, NN) + dot(outer_lo, weight_hi, NN)
        target = dot(coef_hi, value_hi, NN) + dot(coef_hi, value_lo, NN) + dot(coef_lo, value_hi, NN)
        spare = jnp.zeros((2 * LANES - gram.shape[0] - order, LANES), F32)
        tall = jnp.concatenate([gram, target, spare], axis=0)
        turns = LANES // group
        for side in range(2):
            turned = tall[LANES * side : LANES * (side + 1)].T
            for r in range(turns):
                send_ref[pl.ds(turns * side + r, group, stride=8), :] = turned[group * r : group * (r + 1)]

    return kernel


def mode_kernel(arrived_ref, out_ref, *, order):
    total = arrived_ref[0]
    for j in range(1, arrived_ref.shape[0]):
        total = total + arrived_ref[j]
    turns = total.shape[0] // 2
    tall = jnp.concatenate([total, jnp.zeros((LANES - 2 * turns, LANES), F32)], axis=0).T
    after = pltpu.roll(tall, LANES - turns, 1)
    half = order // 2
    gram = jnp.concatenate([tall, after[: half * half]], axis=0)
    target = after[half * half : half * half + order]
    solved = solve_columns(rows_of(gram, order), target)
    lane = lax.broadcasted_iota(jnp.int32, solved.shape, 1)
    solved = jnp.where(lane < turns, solved, 0.0)
    wide = jnp.concatenate([solved, jnp.zeros((LANES - order, LANES), F32)], axis=0).T
    line = wide[0:1]
    for r in range(1, turns):
        line = line + pltpu.roll(wide[0:8], order * r, 1)[r : r + 1]
    out_ref[...] = jnp.broadcast_to(line.reshape(1, 1, LANES), out_ref.shape)


def half_turn_series():
    grid = (np.cos(np.pi * (np.arange(400) + 0.5) / 400) + 1) / 2
    u = np.sqrt(grid) / 2
    sine = np.polynomial.polynomial.polyfit(grid, np.sin(np.pi * u) / u, 4)
    cosine = np.polynomial.polynomial.polyfit(grid, np.cos(np.pi * u), 5)
    return [float(c) * 4.0**k for k, c in enumerate(sine)], [float(c) * 4.0**k for k, c in enumerate(cosine)]


SINE, COSINE = half_turn_series()


def horner(series, x):
    total = x * series[-1] + series[-2]
    for c in series[-3::-1]:
        total = total * x + c
    return total


def basis_kernel(jitter_ref, index_ref, *rest, pieces, near):
    count = len(pieces)
    time_ref = rest[count]
    made = rest[:near] + rest[count + 1 : -1]
    blocks, width = jitter_ref.shape[0], made[0].shape[1] // 2
    tiles = width // LANES
    freqs = (index_ref[...] + 1).astype(F32) / (4.0 * time_ref.shape[0])
    jitter = jnp.concatenate([jitter_ref[...], jnp.zeros((LANES - blocks, LANES), F32)], axis=0).T
    index = lax.broadcasted_iota(jnp.int32, (LANES, LANES), 0)
    for b in range(blocks):
        time_ref[LANES * b : LANES * (b + 1)] = (index + LANES * b).astype(F32) + jitter[:, b : b + 1]
    step = 32

    def copy(c, b):
        at = pl.ds(pl.multiple_of(LANES * b, LANES), LANES)
        return pltpu.make_async_copy(made[c].at[at], rest[c].at[at], rest[-1].at[c - near, b])

    @pl.loop(0, blocks)
    def _(b):
        @pl.loop(0, LANES // step)
        def _(i):
            at = pl.ds(pl.multiple_of(LANES * b + step * i, step), step)
            times = time_ref[at]
            for c in range(count):
                for n in range(tiles):
                    line = pieces[c] * tiles + n
                    cycles = times * freqs[line : line + 1]
                    turn = cycles - ((cycles + NEAREST) - NEAREST)
                    square = turn * turn
                    sine = turn * horner(SINE, square)
                    cosine = horner(COSINE, square)
                    twice = sine + sine
                    start = LANES * n
                    made[c][at, start : start + LANES] = (1.0 - twice * sine).astype(BF16)
                    made[c][at, start + width : start + width + LANES] = (twice * cosine).astype(BF16)

        for c in range(near, count):
            copy(c, b).start()

    @pl.loop(0, blocks)
    def _(b):
        for c in range(near, count):
            copy(c, b).wait()


def final_kernel(place_ref, meta_ref, win_ref, arrived_ref, coef_ref, lc_ref, *rest, group):
    far, (resid_ref, power_ref, res_ref, col_ref, both_ref) = rest[:CHUNKS], rest[CHUNKS : CHUNKS + 5]
    basis_refs, sems = far[:NEAR] + rest[CHUNKS + 5 : -1], rest[-1]
    copies = [None] * (PARTS * NEAR)
    for c in range(NEAR, CHUNKS):
        tall = basis_refs[c].shape[0] // PARTS
        for k in range(PARTS):
            at = pl.ds(tall * k, tall)
            copies.append(pltpu.make_async_copy(far[c].at[at], basis_refs[c].at[at], sems.at[c * PARTS + k]))
            copies[-1].start()
    blocks = win_ref.shape[0]
    order = coef_ref.shape[0]
    rows = meta_ref.shape[1]
    own_rows = rows // 2
    share = power_ref.shape[0]
    same, sigma = window(meta_ref[...])
    modes = natural_modes(arrived_ref[...], blocks, group, order)
    factors = coef_factors(coef_ref[...])
    part = jnp.zeros((rows, LANES), F32)
    seen = jnp.zeros((rows, LANES), F32)
    for b in range(blocks):
        ok, lc = block_of(win_ref, b, own_rows)
        resid = lc - dot(factors, mode_factors(modes[b]), NN)
        res_ref[b] = resid[:own_rows]
        scaled = resid * sigma
        part = part + jnp.where(ok, scaled * scaled, 0.0)
        seen = seen + jnp.where(ok, 1.0, 0.0)
    count = jnp.sum(dot(same, seen.astype(BF16), NN), axis=1, keepdims=True)
    edge = HUBER * spread_of(same, part, count)
    col_ref[0] = jnp.broadcast_to(edge[:own_rows], (own_rows, LANES))
    col_ref[1] = jnp.broadcast_to(sigma[:own_rows], (own_rows, LANES))
    place = place_ref[0]
    ok, lc = own_of(win_ref, place, own_rows)
    resid_ref[...] = lc_ref[...] - (lc - res_ref[place])
    mine = pl.ds(pl.multiple_of(place * share, share), share)
    edge = col_ref[0, mine]
    sigma = col_ref[1, mine]
    total = jnp.zeros((share, LANES), F32)
    level = jnp.zeros((share, LANES), F32)
    for b in range(blocks):
        ok = win_ref[b, mine].astype(F32) < 0.5 * INVALID
        resid = res_ref[b, mine]
        weight = robust_weight(ok, resid * sigma, edge, sigma)
        at = slice(LANES * b, LANES * (b + 1))
        weight_b = weight.astype(BF16)
        value_b = (weight * resid).astype(BF16)
        both_ref[:share, at] = weight_b
        both_ref[share:, at] = value_b
        total = total + weight_b.astype(F32)
        level = level + value_b.astype(F32)
    total = jnp.sum(total, axis=1, keepdims=True)
    level = jnp.sum(level, axis=1, keepdims=True)
    inverse = 1.0 / total
    mean_level = level * inverse
    for c, basis_ref in enumerate(basis_refs):
        width = basis_ref.shape[1] // 2
        for copy in copies[PARTS * c : PARTS * (c + 1)] if c >= NEAR else ():
            copy.wait()
        single = jnp.zeros((2 * share, 2 * width), F32)
        double_cos = [jnp.zeros((share, SLAB), F32) for _ in range(width // SLAB)]
        double_sin = [jnp.zeros((share, SLAB), F32) for _ in range(width // SLAB)]
        for k in range(basis_ref.shape[0] // SLAB):
            at = slice(SLAB * k, SLAB * (k + 1))
            single = single + dot(both_ref[:, at], basis_ref[at], NN)
            for n in range(width // SLAB):
                cos_b = basis_ref[at, SLAB * n : SLAB * (n + 1)]
                sin_b = basis_ref[at, width + SLAB * n : width + SLAB * (n + 1)]
                twice = sin_b + sin_b
                cos_two = 1.0 - twice * sin_b
                sin_two = twice * cos_b
                double_cos[n] = double_cos[n] + dot(both_ref[:share, at], cos_two, NN)
                double_sin[n] = double_sin[n] + dot(both_ref[:share, at], sin_two, NN)
        cosine = single[:share, :width]
        sine = single[:share, width:]
        cosine_two = jnp.concatenate(double_cos, axis=1)
        sine_two = jnp.concatenate(double_sin, axis=1)
        ycos = single[share:, :width] - mean_level * cosine
        ysin = single[share:, width:] - mean_level * sine
        cc_term = 0.5 * (total + cosine_two) - cosine * cosine * inverse + RIDGE * total
        ss_term = 0.5 * (total - cosine_two) - sine * sine * inverse + RIDGE * total
        cs_term = 0.5 * sine_two - cosine * sine * inverse
        determinant = cc_term * ss_term - cs_term * cs_term
        power = (ss_term * ycos * ycos + cc_term * ysin * ysin - 2.0 * cs_term * ycos * ysin) / determinant
        power_ref[:, width * c : width * (c + 1)] = power


def shaped(shape, dtype=F32):
    return jax.ShapeDtypeStruct(shape, dtype)


def call(kernel, out_shape, args, scratch=(), scalar=False, away=(), out_space=pltpu.VMEM, limit=VMEM, name=None):
    specs = [pl.BlockSpec(memory_space=pltpu.HBM if at in away else pltpu.VMEM) for at in range(len(args))]
    if scalar:
        specs[0] = pl.BlockSpec(memory_space=pltpu.SMEM)
    many = isinstance(out_shape, (tuple, list))
    spaces = out_space if isinstance(out_space, (tuple, list)) else [out_space] * (len(out_shape) if many else 1)
    out_specs = [pl.BlockSpec(memory_space=space) for space in spaces]
    return pl.pallas_call(
        kernel,
        out_shape=out_shape,
        in_specs=specs,
        out_specs=out_specs if many else out_specs[0],
        scratch_shapes=list(scratch),
        compiler_params=pltpu.CompilerParams(vmem_limit_bytes=limit),
        name=name,
    )(*args)


def per_device(light_curves, valid, pixel, inv_sigma, modes_init, epoch_jitter, freq_index):
    obj_count = lax.axis_size("obj")
    ep_count = lax.axis_size("ep")
    rows, cols = light_curves.shape
    order = modes_init.shape[1]
    half = rows // 2
    span = ep_count * cols
    group = obj_count
    place = lax.axis_index("ep").astype(jnp.int32)
    places = place.reshape(1)

    fetched = (light_curves, valid, pixel.reshape(1, rows), inv_sigma.reshape(1, rows), modes_init.T)
    fetched = tuple(pltpu.with_memory_space_constraint(a, pltpu.HBM) for a in fetched)
    own, tail, head = call(
        prep_kernel,
        (shaped((2 * rows + 3 * order, cols), BF16), shaped((half + 8, cols)), shaped((half + 8, cols))),
        fetched,
        scratch=[pltpu.VMEM(a.shape, a.dtype) for a in fetched] + [pltpu.SemaphoreType.DMA((5,))],
        away=range(5),
        name="prep",
    )
    ring = [(i, (i + 1) % obj_count) for i in range(obj_count)]
    back = [(i, (i - 1) % obj_count) for i in range(obj_count)]
    left = lax.ppermute(tail, "obj", ring)
    right = lax.ppermute(head, "obj", back)
    shape = (ep_count, 3 * (rows + order), cols)
    wide, meta = call(
        widen_kernel,
        (pltpu.HBM(shape, BF16), shaped((8, 2 * rows))),
        (own, tail, left, right),
        scratch=[pltpu.VMEM(shape[1:], BF16), pltpu.SemaphoreType.DMA((ep_count,))],
        out_space=(pltpu.HBM, pltpu.VMEM),
        name="widen",
    )

    width = freq_index.shape[0] // CHUNKS
    jitter = epoch_jitter.reshape(ep_count, cols)

    index = freq_index.reshape(-1, LANES)

    def basis_of(index):
        size, away = (span, 2 * width), CHUNKS - NEAR
        scratch = [pltpu.VMEM((span, LANES), F32)]
        scratch += [pltpu.VMEM(size, BF16) for _ in range(away)]
        scratch += [pltpu.SemaphoreType.DMA((away, ep_count))]
        return call(
            lambda *refs: basis_kernel(*refs, pieces=range(CHUNKS), near=NEAR),
            [shaped(size, BF16)] * NEAR + [pltpu.HBM(size, BF16)] * away,
            (jitter, index),
            scratch=scratch,
            out_space=[pltpu.VMEM] * NEAR + [pltpu.HBM] * away,
            name="basis",
        )

    wide, index = lax.optimization_barrier((wide, index))
    win = lax.all_to_all(wide, "ep", split_axis=0, concat_axis=0, tiled=True)
    win, *basis = lax.optimization_barrier((win, *basis_of(index)))

    window_rows = 2 * rows
    products = order * order * 3 // 4
    scratch = [
        pltpu.VMEM((ep_count, window_rows, LANES), F32),
        pltpu.VMEM((window_rows, span), BF16),
        pltpu.VMEM((window_rows, span), BF16),
        pltpu.VMEM((window_rows, span), BF16),
        pltpu.VMEM((window_rows, span), BF16),
        pltpu.VMEM((products, span), BF16),
        pltpu.VMEM((products, span), BF16),
        pltpu.VMEM((order, span), BF16),
        pltpu.VMEM((order, span), BF16),
        pltpu.VMEM((ep_count, LANES, LANES), BF16),
    ]
    args = (places, meta, win)
    everyone = ep_count * obj_count
    for iteration in range(ITERS):
        coef_t, send = call(
            make_step_kernel(iteration == 0),
            (shaped((order, window_rows)), shaped((8 * group, LANES))),
            args,
            scratch=scratch,
            scalar=True,
            name=f"objects_{iteration}",
        )
        arrived = lax.all_to_all(
            send.reshape(group, 8, LANES), "obj", split_axis=0, concat_axis=0, tiled=True
        )
        lines = call(
            lambda a, o: mode_kernel(a, o, order=order),
            shaped((everyone, 1, LANES)),
            (arrived,),
            name=f"modes_{iteration}",
        )
        lines = lax.all_to_all(lines, ("ep", "obj"), split_axis=0, concat_axis=0, tiled=True)
        args = (places, meta, win, lines.reshape(everyone, LANES), coef_t)
    basis[NEAR:] = [pltpu.with_memory_space_constraint(b, pltpu.HBM) for b in basis[NEAR:]]
    residual, power = call(
        lambda *refs: final_kernel(*refs, group=group),
        (shaped((rows, cols)), shaped((rows // ep_count, freq_index.shape[0]))),
        (*args, light_curves, *basis),
        scratch=[
            pltpu.VMEM((ep_count, rows, LANES), F32),
            pltpu.VMEM((2, rows, LANES), F32),
            pltpu.VMEM((2 * rows // ep_count, span), BF16),
            *[pltpu.VMEM((span, 2 * width), BF16) for _ in range(NEAR, CHUNKS)],
            pltpu.SemaphoreType.DMA((CHUNKS * PARTS,)),
        ],
        scalar=True,
        away=range(len(args) + 1 + NEAR, len(args) + 1 + CHUNKS),
        limit=32 << 20,
        name="spectrum",
    )
    return residual, power


def solution(mesh):
    in_specs = (P("obj", "ep"), P("obj", "ep"), P("obj"), P("obj"), P("ep", None), P(), P())
    out_specs = (P("obj", "ep"), P(("obj", "ep"), None))
    return jax.shard_map(
        per_device, mesh=mesh, in_specs=in_specs, out_specs=out_specs, check_vma=False
    )
```

```python
import jax
import jax.numpy as jnp
import numpy as np
from jax import lax
from jax.experimental import pallas as pl
from jax.experimental.pallas import tpu as pltpu
from jax.sharding import PartitionSpec as P

ITERS = 2
HUBER = 1.345
DAMP = 2.0
RIDGE = 0.05
INVALID = 1e9
F32 = jnp.float32
BF16 = jnp.bfloat16
LANES = 128
VMEM = 14 << 20
CHUNKS = 4
NEAR = 1
SLAB = 256
PARTS = 4
NEAREST = 1.5 * 2.0**23
NT = (((1,), (1,)), ((), ()))
NN = (((1,), (0,)), ((), ()))


def dot(a, b, dims):
    return lax.dot_general(a, b, dims, preferred_element_type=F32)


def split2(x):
    hi = x.astype(BF16)
    lo = (x - hi.astype(F32)).astype(BF16)
    return hi, lo


def split3(x):
    hi = x.astype(BF16).astype(F32)
    rest = x - hi
    mid = rest.astype(BF16).astype(F32)
    low = (rest - mid).astype(BF16).astype(F32)
    return hi, mid, low


def solve_columns(rows, target):
    order = len(rows)
    half = order // 2
    rows = list(rows)
    scaled = [None] * order
    forward = [None] * order
    for k in range(order):
        at = k if k < half else k - half
        row = rows[k]
        inverse = 1.0 / (row[at : at + 1] + DAMP)
        unit = row * inverse
        scaled[k] = unit
        value = target[k : k + 1] * inverse
        forward[k] = value
        for i in range(k + 1, order):
            here = i if k < half else i - half
            factor = row[here : here + 1]
            if i >= half and k < half:
                rows[i] = rows[i] - factor * unit[half:]
            else:
                rows[i] = rows[i] - factor * unit
        if k < half:
            target = target - row * value
        else:
            target = jnp.concatenate([target[:half], target[half:] - row * value], axis=0)
    width = target.shape[1]
    level = lax.broadcasted_iota(jnp.int32, (half, width), 0)
    upper = jnp.zeros((half, width), F32)
    lower = jnp.zeros((half, width), F32)
    for k in reversed(range(order)):
        unit = scaled[k]
        if k >= half:
            value = forward[k] - jnp.sum(unit * lower, axis=0, keepdims=True)
            lower = jnp.where(level == k - half, value, lower)
        else:
            both = unit[:half] * upper + unit[half:] * lower
            value = forward[k] - jnp.sum(both, axis=0, keepdims=True)
            upper = jnp.where(level == k, value, upper)
    return jnp.concatenate([upper, lower], axis=0)


def outer_rows(x):
    half = x.shape[0] // 2
    upper = [x[i : i + 1] * x for i in range(half)]
    lower = [x[i : i + 1] * x[half:] for i in range(half, 2 * half)]
    return jnp.concatenate(upper + lower, axis=0)


def rows_of(gram, order):
    half = order // 2
    top = [gram[order * i : order * (i + 1)] for i in range(half)]
    start = order * half
    return top + [gram[start + half * i : start + half * (i + 1)] for i in range(half)]


def coef_factors(coef_t):
    order = coef_t.shape[0]
    hi, mid, low = split3(coef_t)
    none = jnp.zeros((LANES - 6 * order, coef_t.shape[1]), F32)
    stack = jnp.concatenate([hi, mid, low, hi, mid, hi, none], axis=0)
    return stack.T.astype(BF16)


def mode_factors(modes_b):
    order = modes_b.shape[0]
    hi, mid, low = split3(modes_b)
    none = jnp.zeros((LANES - 6 * order, modes_b.shape[1]), F32)
    return jnp.concatenate([hi, hi, hi, mid, mid, low, none], axis=0).astype(BF16)


def window(meta):
    rows = meta.shape[1]
    filled = jnp.concatenate([meta, jnp.zeros((LANES - meta.shape[0], rows), F32)], axis=0)
    turned = filled.T
    same = (turned[:, 0:1] == meta[0:1]).astype(F32).astype(BF16)
    return same, turned[:, 1:2]


def own_of(win_ref, b, rows):
    coded = win_ref[b, :rows].astype(F32) + win_ref[b, rows : 2 * rows].astype(F32)
    ok = coded < 0.5 * INVALID
    return ok, jnp.where(ok, coded, 0.0)


def block_of(win_ref, b, rows):
    own = win_ref[b, :rows].astype(F32) + win_ref[b, rows : 2 * rows].astype(F32)
    coded = jnp.concatenate([own, win_ref[b, 2 * rows : 3 * rows].astype(F32)], axis=0)
    ok = coded < 0.5 * INVALID
    return ok, jnp.where(ok, coded, 0.0)


def first_modes(win_ref, b, rows, order):
    parts = win_ref[b, 3 * rows :].astype(F32)
    return parts[:order] + (parts[order : 2 * order] + parts[2 * order :])


def pixel_total(same, part):
    hi, mid, low = split3(part)
    wide = jnp.concatenate([hi, mid, low], axis=1).astype(BF16)
    total = dot(same, wide, NN)
    total = total[:, :LANES] + total[:, LANES : 2 * LANES] + total[:, 2 * LANES :]
    return jnp.sum(total, axis=1, keepdims=True)


def spread_of(same, part, count):
    return jnp.sqrt(pixel_total(same, part) / jnp.maximum(count, 1.0) + 1e-06)


def robust_weight(ok, scaled, edge, sigma):
    return jnp.where(ok, (sigma * sigma) * (edge / jnp.maximum(jnp.abs(scaled), edge)), 0.0)


def natural_modes(arrived, blocks, group, order):
    turns = LANES // group
    lane = lax.broadcasted_iota(jnp.int32, (order, LANES), 1)
    turned = arrived.T
    out = []
    for b in range(blocks):
        tile, inner = divmod(b * group, LANES)
        total = jnp.zeros((order, LANES), F32)
        for r in range(turns):
            piece = turned[order * r : order * (r + 1), LANES * tile : LANES * (tile + 1)]
            shift = (group * r - inner) % LANES
            if shift:
                piece = pltpu.roll(piece, shift, 1)
            inside = (lane >= group * r) & (lane < group * (r + 1))
            total = jnp.where(inside, piece, total)
        out.append(total)
    return out


def prep_kernel(lc_hbm, valid_hbm, pix_hbm, sig_hbm, init_hbm, own_ref, tail_ref, head_ref,
                lc_ref, valid_ref, pix_ref, sig_ref, init_ref, sems):
    pairs = (
        (lc_hbm, lc_ref), (valid_hbm, valid_ref), (pix_hbm, pix_ref), (sig_hbm, sig_ref), (init_hbm, init_ref)
    )
    copies = [pltpu.make_async_copy(a, b, sems.at[i]) for i, (a, b) in enumerate(pairs)]
    for copy in copies:
        copy.start()
    for copy in copies:
        copy.wait()
    rows = lc_ref.shape[0]
    half = rows // 2
    coded = jnp.where(valid_ref[...] != 0, lc_ref[...], INVALID)
    own_ref[:rows], own_ref[rows : 2 * rows] = split2(coded)
    own_ref[2 * rows :] = jnp.concatenate(split3(init_ref[...]), axis=0).astype(BF16)
    meta = jnp.concatenate(
        [pix_ref[...].astype(F32), sig_ref[...], jnp.zeros((6, rows), F32)], axis=0
    )
    tail_ref[:half] = coded[half:]
    tail_ref[half:] = meta
    head_ref[:half] = coded[:half]
    head_ref[half:] = meta


def widen_kernel(own_ref, tail_ref, left_ref, right_ref, out_hbm, meta_ref, one_ref, sems):
    rows = tail_ref.shape[1]
    half = rows // 2
    left = left_ref[...]
    right = right_ref[...]
    one_ref[: 2 * rows] = own_ref[: 2 * rows]
    one_ref[2 * rows : 3 * rows] = jnp.concatenate([left[:half], right[:half]], axis=0).astype(BF16)
    one_ref[3 * rows :] = own_ref[2 * rows :]
    copies = [pltpu.make_async_copy(one_ref, out_hbm.at[b], sems.at[b]) for b in range(out_hbm.shape[0])]
    for copy in copies:
        copy.start()
    lane = lax.broadcasted_iota(jnp.int32, (8, rows), 1)
    beyond = pltpu.roll(jnp.where(lane >= half, left[half:], right[half:]), half, 1)
    meta_ref[:, :rows] = tail_ref[half:]
    meta_ref[:, rows:] = beyond
    for copy in copies:
        copy.wait()


def make_step_kernel(first):
    def kernel(*refs):
        if first:
            place_ref, meta_ref, win_ref = refs[:3]
            rest = refs[3:]
        else:
            place_ref, meta_ref, win_ref, arrived_ref, before_ref = refs[:5]
            rest = refs[5:]
        coef_ref, send_ref, scal_ref, wh_ref, wl_ref, ph_ref, pl_ref, oh_ref, ol_ref, mh_ref, ml_ref, ms_ref = rest
        blocks = win_ref.shape[0]
        order = coef_ref.shape[0]
        rows = meta_ref.shape[1]
        own_rows = rows // 2
        group = send_ref.shape[0] // 8
        same, sigma = window(meta_ref[...])
        if first:
            modes = [first_modes(win_ref, b, own_rows, order) for b in range(blocks)]
        else:
            modes = natural_modes(arrived_ref[...], blocks, group, order)
            factors = coef_factors(before_ref[...])
        part = jnp.zeros((rows, LANES), F32)
        seen = jnp.zeros((rows, LANES), F32)
        for b in range(blocks):
            ok, lc = block_of(win_ref, b, own_rows)
            ms_ref[b] = mode_factors(modes[b])
            if not first:
                lc = lc - dot(factors, ms_ref[b], NN)
            scaled = lc * sigma
            scal_ref[b] = scaled
            part = part + jnp.where(ok, scaled * scaled, 0.0)
            seen = seen + jnp.where(ok, 1.0, 0.0)
        count = jnp.sum(dot(same, seen.astype(BF16), NN), axis=1, keepdims=True)
        edge = HUBER * spread_of(same, part, count)
        for b in range(blocks):
            ok, lc = block_of(win_ref, b, own_rows)
            weight = robust_weight(ok, scal_ref[b], edge, sigma)
            at = slice(LANES * b, LANES * (b + 1))
            wh_ref[:, at], wl_ref[:, at] = split2(weight)
            ph_ref[:, at], pl_ref[:, at] = split2(weight * lc)
            oh_ref[:, at], ol_ref[:, at] = split2(outer_rows(modes[b]))
            mh_ref[:, at], ml_ref[:, at] = split2(modes[b])
        gram = (
            dot(oh_ref[...], wh_ref[...], NT)
            + dot(oh_ref[...], wl_ref[...], NT)
            + dot(ol_ref[...], wh_ref[...], NT)
        )
        target = (
            dot(mh_ref[...], ph_ref[...], NT)
            + dot(mh_ref[...], pl_ref[...], NT)
            + dot(ml_ref[...], ph_ref[...], NT)
        )
        coef_t = solve_columns(rows_of(gram, order), target)
        coef_ref[...] = coef_t
        factors = coef_factors(coef_t)
        part = jnp.zeros((rows, LANES), F32)
        for b in range(blocks):
            ok, lc = block_of(win_ref, b, own_rows)
            scaled = (lc - dot(factors, ms_ref[b], NN)) * sigma
            scal_ref[b] = scaled
            part = part + jnp.where(ok, scaled * scaled, 0.0)
        edge = HUBER * spread_of(same, part, count)
        place = place_ref[0]
        ok, lc = own_of(win_ref, place, own_rows)
        weight = robust_weight(ok, scal_ref[place, :own_rows], edge[:own_rows], sigma[:own_rows])
        weight_hi, weight_lo = split2(weight)
        value_hi, value_lo = split2(weight * lc)
        own_coef = coef_t[:, :own_rows]
        outer_hi, outer_lo = split2(outer_rows(own_coef))
        coef_hi, coef_lo = split2(own_coef)
        gram = dot(outer_hi, weight_hi, NN) + dot(outer_hi, weight_lo, NN) + dot(outer_lo, weight_hi, NN)
        target = dot(coef_hi, value_hi, NN) + dot(coef_hi, value_lo, NN) + dot(coef_lo, value_hi, NN)
        spare = jnp.zeros((2 * LANES - gram.shape[0] - order, LANES), F32)
        tall = jnp.concatenate([gram, target, spare], axis=0)
        turns = LANES // group
        for side in range(2):
            turned = tall[LANES * side : LANES * (side + 1)].T
            for r in range(turns):
                send_ref[pl.ds(turns * side + r, group, stride=8), :] = turned[group * r : group * (r + 1)]

    return kernel


def mode_kernel(arrived_ref, out_ref, *, order):
    total = arrived_ref[0]
    for j in range(1, arrived_ref.shape[0]):
        total = total + arrived_ref[j]
    turns = total.shape[0] // 2
    tall = jnp.concatenate([total, jnp.zeros((LANES - 2 * turns, LANES), F32)], axis=0).T
    after = pltpu.roll(tall, LANES - turns, 1)
    half = order // 2
    gram = jnp.concatenate([tall, after[: half * half]], axis=0)
    target = after[half * half : half * half + order]
    solved = solve_columns(rows_of(gram, order), target)
    lane = lax.broadcasted_iota(jnp.int32, solved.shape, 1)
    solved = jnp.where(lane < turns, solved, 0.0)
    wide = jnp.concatenate([solved, jnp.zeros((LANES - order, LANES), F32)], axis=0).T
    line = wide[0:1]
    for r in range(1, turns):
        line = line + pltpu.roll(wide[0:8], order * r, 1)[r : r + 1]
    out_ref[...] = jnp.broadcast_to(line.reshape(1, 1, LANES), out_ref.shape)


def half_turn_series():
    grid = (np.cos(np.pi * (np.arange(400) + 0.5) / 400) + 1) / 2
    u = np.sqrt(grid) / 2
    sine = np.polynomial.polynomial.polyfit(grid, np.sin(np.pi * u) / u, 4)
    cosine = np.polynomial.polynomial.polyfit(grid, np.cos(np.pi * u), 4)
    return [float(c) * 4.0**k for k, c in enumerate(sine)], [float(c) * 4.0**k for k, c in enumerate(cosine)]


SINE, COSINE = half_turn_series()


def horner(series, x):
    total = x * series[-1] + series[-2]
    for c in series[-3::-1]:
        total = total * x + c
    return total


def basis_kernel(jitter_ref, index_ref, *rest, pieces, near):
    count = len(pieces)
    time_ref = rest[count]
    made = rest[:near] + rest[count + 1 : -1]
    blocks, width = jitter_ref.shape[0], made[0].shape[1] // 2
    tiles = width // LANES
    freqs = (index_ref[...] + 1).astype(F32) / (4.0 * time_ref.shape[0])
    jitter = jnp.concatenate([jitter_ref[...], jnp.zeros((LANES - blocks, LANES), F32)], axis=0).T
    index = lax.broadcasted_iota(jnp.int32, (LANES, LANES), 0)
    for b in range(blocks):
        time_ref[LANES * b : LANES * (b + 1)] = (index + LANES * b).astype(F32) + jitter[:, b : b + 1]
    step = 64

    def copy(c, b):
        at = pl.ds(pl.multiple_of(LANES * b, LANES), LANES)
        return pltpu.make_async_copy(made[c].at[at], rest[c].at[at], rest[-1].at[c - near, b])

    @pl.loop(0, blocks)
    def _(b):
        @pl.loop(0, LANES // step)
        def _(i):
            at = pl.ds(pl.multiple_of(LANES * b + step * i, step), step)
            times = time_ref[at]
            for c in range(count):
                for n in range(tiles):
                    line = pieces[c] * tiles + n
                    cycles = times * freqs[line : line + 1]
                    turn = cycles - ((cycles + NEAREST) - NEAREST)
                    square = turn * turn
                    sine = turn * horner(SINE, square)
                    cosine = horner(COSINE, square)
                    twice = sine + sine
                    start = LANES * n
                    made[c][at, start : start + LANES] = (1.0 - twice * sine).astype(BF16)
                    made[c][at, start + width : start + width + LANES] = (twice * cosine).astype(BF16)

        for c in range(near, count):
            copy(c, b).start()

    @pl.loop(0, blocks)
    def _(b):
        for c in range(near, count):
            copy(c, b).wait()


def final_kernel(place_ref, meta_ref, win_ref, arrived_ref, coef_ref, lc_ref, *rest, group):
    far, (resid_ref, power_ref, res_ref, col_ref, both_ref) = rest[:CHUNKS], rest[CHUNKS : CHUNKS + 5]
    basis_refs, sems = far[:NEAR] + rest[CHUNKS + 5 : -1], rest[-1]
    copies = [None] * (PARTS * NEAR)
    for c in range(NEAR, CHUNKS):
        tall = basis_refs[c].shape[0] // PARTS
        for k in range(PARTS):
            at = pl.ds(tall * k, tall)
            copies.append(pltpu.make_async_copy(far[c].at[at], basis_refs[c].at[at], sems.at[c * PARTS + k]))
            copies[-1].start()
    blocks = win_ref.shape[0]
    order = coef_ref.shape[0]
    rows = meta_ref.shape[1]
    own_rows = rows // 2
    share = power_ref.shape[0]
    same, sigma = window(meta_ref[...])
    modes = natural_modes(arrived_ref[...], blocks, group, order)
    factors = coef_factors(coef_ref[...])
    part = jnp.zeros((rows, LANES), F32)
    seen = jnp.zeros((rows, LANES), F32)
    for b in range(blocks):
        ok, lc = block_of(win_ref, b, own_rows)
        resid = lc - dot(factors, mode_factors(modes[b]), NN)
        res_ref[b] = resid[:own_rows]
        scaled = resid * sigma
        part = part + jnp.where(ok, scaled * scaled, 0.0)
        seen = seen + jnp.where(ok, 1.0, 0.0)
    count = jnp.sum(dot(same, seen.astype(BF16), NN), axis=1, keepdims=True)
    edge = HUBER * spread_of(same, part, count)
    col_ref[0] = jnp.broadcast_to(edge[:own_rows], (own_rows, LANES))
    col_ref[1] = jnp.broadcast_to(sigma[:own_rows], (own_rows, LANES))
    place = place_ref[0]
    ok, lc = own_of(win_ref, place, own_rows)
    resid_ref[...] = lc_ref[...] - (lc - res_ref[place])
    mine = pl.ds(pl.multiple_of(place * share, share), share)
    edge = col_ref[0, mine]
    sigma = col_ref[1, mine]
    total = jnp.zeros((share, LANES), F32)
    level = jnp.zeros((share, LANES), F32)
    for b in range(blocks):
        ok = win_ref[b, mine].astype(F32) < 0.5 * INVALID
        resid = res_ref[b, mine]
        weight = robust_weight(ok, resid * sigma, edge, sigma)
        at = slice(LANES * b, LANES * (b + 1))
        weight_b = weight.astype(BF16)
        value_b = (weight * resid).astype(BF16)
        both_ref[:share, at] = weight_b
        both_ref[share:, at] = value_b
        total = total + weight_b.astype(F32)
        level = level + value_b.astype(F32)
    total = jnp.sum(total, axis=1, keepdims=True)
    level = jnp.sum(level, axis=1, keepdims=True)
    inverse = 1.0 / total
    mean_level = level * inverse
    for c, basis_ref in enumerate(basis_refs):
        width = basis_ref.shape[1] // 2
        for copy in copies[PARTS * c : PARTS * (c + 1)] if c >= NEAR else ():
            copy.wait()
        single = jnp.zeros((2 * share, 2 * width), F32)
        double_cos = [jnp.zeros((share, SLAB), F32) for _ in range(width // SLAB)]
        double_sin = [jnp.zeros((share, SLAB), F32) for _ in range(width // SLAB)]
        for k in range(basis_ref.shape[0] // SLAB):
            at = slice(SLAB * k, SLAB * (k + 1))
            single = single + dot(both_ref[:, at], basis_ref[at], NN)
            for n in range(width // SLAB):
                cos_b = basis_ref[at, SLAB * n : SLAB * (n + 1)]
                sin_b = basis_ref[at, width + SLAB * n : width + SLAB * (n + 1)]
                twice = sin_b + sin_b
                cos_two = 1.0 - twice * sin_b
                sin_two = twice * cos_b
                double_cos[n] = double_cos[n] + dot(both_ref[:share, at], cos_two, NN)
                double_sin[n] = double_sin[n] + dot(both_ref[:share, at], sin_two, NN)
        cosine = single[:share, :width]
        sine = single[:share, width:]
        cosine_two = jnp.concatenate(double_cos, axis=1)
        sine_two = jnp.concatenate(double_sin, axis=1)
        ycos = single[share:, :width] - mean_level * cosine
        ysin = single[share:, width:] - mean_level * sine
        cc_term = 0.5 * (total + cosine_two) - cosine * cosine * inverse + RIDGE * total
        ss_term = 0.5 * (total - cosine_two) - sine * sine * inverse + RIDGE * total
        cs_term = 0.5 * sine_two - cosine * sine * inverse
        determinant = cc_term * ss_term - cs_term * cs_term
        power = (ss_term * ycos * ycos + cc_term * ysin * ysin - 2.0 * cs_term * ycos * ysin) / determinant
        power_ref[:, width * c : width * (c + 1)] = power


def shaped(shape, dtype=F32):
    return jax.ShapeDtypeStruct(shape, dtype)


def call(kernel, out_shape, args, scratch=(), scalar=False, away=(), out_space=pltpu.VMEM, limit=VMEM, name=None):
    specs = [pl.BlockSpec(memory_space=pltpu.HBM if at in away else pltpu.VMEM) for at in range(len(args))]
    if scalar:
        specs[0] = pl.BlockSpec(memory_space=pltpu.SMEM)
    many = isinstance(out_shape, (tuple, list))
    spaces = out_space if isinstance(out_space, (tuple, list)) else [out_space] * (len(out_shape) if many else 1)
    out_specs = [pl.BlockSpec(memory_space=space) for space in spaces]
    return pl.pallas_call(
        kernel,
        out_shape=out_shape,
        in_specs=specs,
        out_specs=out_specs if many else out_specs[0],
        scratch_shapes=list(scratch),
        compiler_params=pltpu.CompilerParams(vmem_limit_bytes=limit),
        name=name,
    )(*args)


def per_device(light_curves, valid, pixel, inv_sigma, modes_init, epoch_jitter, freq_index):
    obj_count = lax.axis_size("obj")
    ep_count = lax.axis_size("ep")
    rows, cols = light_curves.shape
    order = modes_init.shape[1]
    half = rows // 2
    span = ep_count * cols
    group = obj_count
    place = lax.axis_index("ep").astype(jnp.int32)
    places = place.reshape(1)

    fetched = (light_curves, valid, pixel.reshape(1, rows), inv_sigma.reshape(1, rows), modes_init.T)
    fetched = tuple(pltpu.with_memory_space_constraint(a, pltpu.HBM) for a in fetched)
    own, tail, head = call(
        prep_kernel,
        (shaped((2 * rows + 3 * order, cols), BF16), shaped((half + 8, cols)), shaped((half + 8, cols))),
        fetched,
        scratch=[pltpu.VMEM(a.shape, a.dtype) for a in fetched] + [pltpu.SemaphoreType.DMA((5,))],
        away=range(5),
        name="prep",
    )
    ring = [(i, (i + 1) % obj_count) for i in range(obj_count)]
    back = [(i, (i - 1) % obj_count) for i in range(obj_count)]
    left = lax.ppermute(tail, "obj", ring)
    right = lax.ppermute(head, "obj", back)
    shape = (ep_count, 3 * (rows + order), cols)
    wide, meta = call(
        widen_kernel,
        (pltpu.HBM(shape, BF16), shaped((8, 2 * rows))),
        (own, tail, left, right),
        scratch=[pltpu.VMEM(shape[1:], BF16), pltpu.SemaphoreType.DMA((ep_count,))],
        out_space=(pltpu.HBM, pltpu.VMEM),
        name="widen",
    )

    width = freq_index.shape[0] // CHUNKS
    jitter = epoch_jitter.reshape(ep_count, cols)

    index = freq_index.reshape(-1, LANES)

    def basis_of(index):
        size, away = (span, 2 * width), CHUNKS - NEAR
        scratch = [pltpu.VMEM((span, LANES), F32)]
        scratch += [pltpu.VMEM(size, BF16) for _ in range(away)]
        scratch += [pltpu.SemaphoreType.DMA((away, ep_count))]
        return call(
            lambda *refs: basis_kernel(*refs, pieces=range(CHUNKS), near=NEAR),
            [shaped(size, BF16)] * NEAR + [pltpu.HBM(size, BF16)] * away,
            (jitter, index),
            scratch=scratch,
            out_space=[pltpu.VMEM] * NEAR + [pltpu.HBM] * away,
            name="basis",
        )

    wide, index = lax.optimization_barrier((wide, index))
    win = lax.all_to_all(wide, "ep", split_axis=0, concat_axis=0, tiled=True)
    win, *basis = lax.optimization_barrier((win, *basis_of(index)))

    window_rows = 2 * rows
    products = order * order * 3 // 4
    scratch = [
        pltpu.VMEM((ep_count, window_rows, LANES), F32),
        pltpu.VMEM((window_rows, span), BF16),
        pltpu.VMEM((window_rows, span), BF16),
        pltpu.VMEM((window_rows, span), BF16),
        pltpu.VMEM((window_rows, span), BF16),
        pltpu.VMEM((products, span), BF16),
        pltpu.VMEM((products, span), BF16),
        pltpu.VMEM((order, span), BF16),
        pltpu.VMEM((order, span), BF16),
        pltpu.VMEM((ep_count, LANES, LANES), BF16),
    ]
    args = (places, meta, win)
    everyone = ep_count * obj_count
    for iteration in range(ITERS):
        coef_t, send = call(
            make_step_kernel(iteration == 0),
            (shaped((order, window_rows)), shaped((8 * group, LANES))),
            args,
            scratch=scratch,
            scalar=True,
            name=f"objects_{iteration}",
        )
        arrived = lax.all_to_all(
            send.reshape(group, 8, LANES), "obj", split_axis=0, concat_axis=0, tiled=True
        )
        lines = call(
            lambda a, o: mode_kernel(a, o, order=order),
            shaped((everyone, 1, LANES)),
            (arrived,),
            name=f"modes_{iteration}",
        )
        lines = lax.all_to_all(lines, ("ep", "obj"), split_axis=0, concat_axis=0, tiled=True)
        args = (places, meta, win, lines.reshape(everyone, LANES), coef_t)
    basis[NEAR:] = [pltpu.with_memory_space_constraint(b, pltpu.HBM) for b in basis[NEAR:]]
    residual, power = call(
        lambda *refs: final_kernel(*refs, group=group),
        (shaped((rows, cols)), shaped((rows // ep_count, freq_index.shape[0]))),
        (*args, light_curves, *basis),
        scratch=[
            pltpu.VMEM((ep_count, rows, LANES), F32),
            pltpu.VMEM((2, rows, LANES), F32),
            pltpu.VMEM((2 * rows // ep_count, span), BF16),
            *[pltpu.VMEM((span, 2 * width), BF16) for _ in range(NEAR, CHUNKS)],
            pltpu.SemaphoreType.DMA((CHUNKS * PARTS,)),
        ],
        scalar=True,
        away=range(len(args) + 1 + NEAR, len(args) + 1 + CHUNKS),
        limit=32 << 20,
        name="spectrum",
    )
    return residual, power


def solution(mesh):
    in_specs = (P("obj", "ep"), P("obj", "ep"), P("obj"), P("obj"), P("ep", None), P(), P())
    out_specs = (P("obj", "ep"), P(("obj", "ep"), None))
    return jax.shard_map(
        per_device, mesh=mesh, in_specs=in_specs, out_specs=out_specs, check_vma=False
    )
```
